32 devices in a mesh: grp: 2 (over y), tm: 4 (over z), seq: 2 (over x), sub: 2 (over core).
Axes of the slice: x: 2, y: 2, z: 4, core: 2. Of those that a mesh axis runs over, the one named last changes fastest.
Arguments:
- queries: bfloat16 [4, 2048, 768], P(('grp', 'seq'), 'tm', 'sub'), parts along dimension 0, may hold values from -6 to 6
- key_proj: bfloat16 [4, 2048, 768], P(('grp', 'seq'), 'tm', 'sub'), parts along dimension 0, may hold values from -6 to 6
- value_proj: bfloat16 [4, 2048, 768], P(('grp', 'seq'), 'tm', 'sub'), parts along dimension 0, may hold values from -6 to 6
- residual: bfloat16 [4, 2048, 768], P(('grp', 'seq'), 'tm'), parts along dimension 0, may hold values from -3 to 3
- mix_weight: bfloat16 [768, 768], P('sub', 'seq'), may hold values from -0.875 to 0.875
- inner_weight: bfloat16 [768, 1536], P('seq', 'sub'), may hold values from -0.21875 to 0.21875
- write_weight: bfloat16 [768, 128], P('seq'), may hold values from -0.046875 to 0.046875
- read_weight: bfloat16 [768, 128], P('seq'), may hold values from -0.0234375 to 0.0234375
- step_logits: float32 [4, 24, 2048], P(('grp', 'seq'), 'sub', 'tm'), parts along dimension 0
- decay_rates: float32 [24], P('sub'), as said below
- carried_state: float32 [4, 24, 64, 128], P(('grp', 'seq'), 'sub'), parts along dimension 0, may hold values from -6 to 6
- carried_valid: int32 [4, 24], P(('grp', 'seq'), 'sub'), parts along dimension 0, may hold values 0 or 1
Outputs:
- stream: bfloat16 [4, 2048, 768], P(('grp', 'seq'), 'tm'), parts along dimension 0
- scan_out: bfloat16 [4, 2048, 1536], P(('grp', 'seq'), 'tm', 'sub'), parts along dimension 0
The draws below stay inside these ranges and needn't reach their ends.
There are 2 independent parts, one for each index of `grp`. The reference program is written for one: setup_inputs(seed, part) draws one part's arguments, and reference() takes and returns one part's arrays. A program takes and returns all parts, laid end to end along the dimension named above; an argument that names none is the same for every part. Nothing has to cross between parts.
Inputs may be any that keep to these rules, and one draw needn't show every extreme that they name: `decay_rates`: positive.
All inputs are finite; a program needn't handle non-finite values. No bound on the sum of `carried_valid` on one device may be relied on, other than what follows from the above.
Results may differ from the reference program's by a relative error of at most 0.025.
Values may be sent and summed in bfloat16 or wider, within the bound.
A program may use at most 64 MiB of HBM per device.

```python
import math
import jax
import jax.numpy as jnp
from jax import lax

WIDTH = 768
HEADS = 12
HEAD_DIM = 64
SSM_HEADS = 24
SSM_DIM = 64
STATE = 128
STRIDE = 256
STRETCH = 128
TOK_DEV = 512
SEQUENCE_COUNT = 2
SAMPLE_LENGTH = 2048


def anchor_layout(key):
    signs = jax.random.rademacher(jax.random.fold_in(key, 11), (HEADS, HEAD_DIM)).astype(jnp.float32)
    sample_positions = jnp.arange(SAMPLE_LENGTH, dtype=jnp.int32)
    period = 2 * STRIDE
    anchor = sample_positions % period == STRIDE + 5
    beside = ((sample_positions + 1) % period == STRIDE + 5) | ((sample_positions + STRIDE) % period == STRIDE + 5)
    strength = 4.5 + 0.5 * (sample_positions // period % 4).astype(jnp.float32)
    return (signs, anchor, beside, strength)


def base_values(key, salt):
    shape = (SEQUENCE_COUNT, SAMPLE_LENGTH, HEADS, HEAD_DIM)
    return jnp.clip(jax.random.normal(jax.random.fold_in(key, salt), shape), -4.0, 4.0)


def draw_queries(key, part):
    signs, anchor, beside, strength = anchor_layout(key)
    base = base_values(key, 1)
    aligned = strength[None, :, None, None] * signs[None, None]
    value_entry = jnp.where(anchor[None, :, None, None], aligned, base)
    return value_entry.reshape(SEQUENCE_COUNT, SAMPLE_LENGTH, HEADS * HEAD_DIM).astype(jnp.bfloat16)


def draw_key_proj(key, part):
    signs, anchor, beside, strength = anchor_layout(key)
    base = base_values(key, 2)
    aligned = strength[None, :, None, None] * signs[None, None]
    nearly = (strength - 0.05)[None, :, None, None] * signs[None, None]
    value_entry = jnp.where(anchor[None, :, None, None], aligned, jnp.where(beside[None, :, None, None], nearly, base))
    return value_entry.reshape(SEQUENCE_COUNT, SAMPLE_LENGTH, HEADS * HEAD_DIM).astype(jnp.bfloat16)


def draw_step_logits(key, part):
    shape = (SEQUENCE_COUNT, SSM_HEADS, SAMPLE_LENGTH)
    noise = jnp.clip(jax.random.normal(jax.random.fold_in(key, 31), shape), -3.0, 3.0)
    offset = jax.random.uniform(jax.random.fold_in(key, 32), (SEQUENCE_COUNT, SSM_HEADS, SAMPLE_LENGTH // TOK_DEV), minval=-0.7, maxval=0.7)
    offset = jnp.repeat(offset, TOK_DEV, axis=2)
    pulse_window_start = jax.random.randint(jax.random.fold_in(key, 33), (SEQUENCE_COUNT, 3), 0, SAMPLE_LENGTH)
    sample_positions = jnp.arange(SAMPLE_LENGTH, dtype=jnp.int32)
    pulse_window = jnp.any(sample_positions[None, None, :] == pulse_window_start[:, :, None], axis=1)
    value_entry = -2.0 + 0.7 * noise + offset
    return jnp.where(pulse_window[:, None, :], SAMPLE_LENGTH / 16.0, value_entry).astype(jnp.float32)


def draw_decay_rates(key, part):
    pick = jax.random.uniform(jax.random.fold_in(key, 41), (SSM_HEADS,))
    slow = jnp.exp(jax.random.uniform(jax.random.fold_in(key, 42), (SSM_HEADS,), minval=math.log(3.0), maxval=math.log(6.0))) / SAMPLE_LENGTH
    fast = jnp.exp(jax.random.uniform(jax.random.fold_in(key, 43), (SSM_HEADS,), minval=math.log(0.13), maxval=math.log(0.2)))
    share = 0.5
    return jnp.where(pick < share, slow, fast).astype(jnp.float32)


def plant(entries, own_key, smallest, top_value):
    shape = entries.shape
    index_at = [jax.random.randint(jax.random.fold_in(own_key, axis), (), 0, shape[axis]) for axis in range(len(shape))]
    entries = entries.at[tuple(index_at)].set(smallest)
    longest = shape.index(max(shape))
    index_at[longest] = (index_at[longest] + 1) % shape[longest]
    return entries.at[tuple(index_at)].set(top_value)


def levels(key, shape, pieces, least, largest):
    loudness, own = 1.0, jax.random.fold_in(key, 6)
    for dim, shards_of in pieces:
        draws = jnp.exp(jax.random.uniform(jax.random.fold_in(own, dim), (shards_of,), jnp.float32, least / len(pieces), largest / len(pieces)))
        loudness = loudness * jnp.repeat(draws, shape[dim] // shards_of).reshape([-1 if axis == dim else 1 for axis in range(len(shape))])
    return loudness


def gaussian(key, extent, scale, bound, pieces=(), held_as=jnp.bfloat16):
    gain = levels(key, extent, pieces, -0.22, 0.18) if pieces else 1.0
    drawn = jax.random.normal(key, extent, jnp.float32) * scale * gain
    return jnp.minimum(jnp.maximum(drawn, -bound), bound).astype(held_as)


def setup_inputs(seed: int = 0, part: int = 0) -> dict:
    seeds = jax.random.split(jax.random.key(seed), 13)
    own_keys = jax.random.split(jax.random.fold_in(seeds[12], part), 13)
    queries = draw_queries(jax.random.fold_in(jax.random.fold_in(seeds[12], part), 71), part)
    key_proj = draw_key_proj(jax.random.fold_in(jax.random.fold_in(seeds[12], part), 71), part)
    value_proj = gaussian(own_keys[2], (SEQUENCE_COUNT, SAMPLE_LENGTH, HEADS * HEAD_DIM), 1.0, 6.0, ((0, 2), (1, 4), (2, 2)))
    residual = gaussian(own_keys[3], (SEQUENCE_COUNT, SAMPLE_LENGTH, WIDTH), 0.5, 3.0, ((0, 2), (1, 4)))
    mix_weight = gaussian(seeds[4], (HEADS * HEAD_DIM, WIDTH), (HEADS * HEAD_DIM // 16) ** -0.5, 0.875, ((0, 2), (1, 2)))
    inner_weight = gaussian(seeds[5], (WIDTH, SSM_HEADS * SSM_DIM), WIDTH ** -0.5, 0.21875, ((0, 2), (1, 2)))
    write_weight = gaussian(seeds[6], (WIDTH, STATE), (25 * WIDTH) ** -0.5, 0.046875, ((0, 2),))
    read_weight = gaussian(seeds[7], (WIDTH, STATE), (100 * WIDTH) ** -0.5, 0.0234375, ((0, 2),))
    step_logits = draw_step_logits(jax.random.fold_in(jax.random.fold_in(seeds[12], part), 71), part)
    decay_rates = draw_decay_rates(jax.random.fold_in(seeds[12], 71), part)
    carried_state = gaussian(own_keys[10], (SEQUENCE_COUNT, SSM_HEADS, SSM_DIM, STATE), 1.0, 6.0, ((0, 2), (1, 2)), jnp.float32)
    carried_valid = plant((jax.random.randint(own_keys[11], (SEQUENCE_COUNT, SSM_HEADS), 0, 2) < 1).astype(jnp.int32), jax.random.fold_in(own_keys[11], 1), 0, 1)
    return {"queries": queries, "key_proj": key_proj, "value_proj": value_proj, "residual": residual, "mix_weight": mix_weight, "inner_weight": inner_weight, "write_weight": write_weight, "read_weight": read_weight, "step_logits": step_logits, "decay_rates": decay_rates, "carried_state": carried_state, "carried_valid": carried_valid}


SCALE = 0.125
NEGATIVE = -1e+30
EPSILON = 1e-05
HIGHEST = lax.Precision.HIGHEST

def softmax_rows(scores, allowed):
    scores = jnp.where(allowed, scores, NEGATIVE)
    row_max = lax.optimization_barrier(jnp.max(scores, axis=-1, keepdims=True))
    weights = jnp.where(allowed, jnp.exp(scores - row_max), 0.0)
    weight_sum = lax.optimization_barrier(jnp.sum(weights, axis=-1))
    rounded = lax.optimization_barrier(weights.astype(jnp.bfloat16)).astype(jnp.float32)
    return (rounded, weight_sum)

def near_attention(query_rows, key_rows, value_rows):
    length = query_rows.shape[0]
    padding = jnp.zeros((STRIDE,) + key_rows.shape[1:], key_rows.dtype)
    key_padded = jnp.concatenate([padding, key_rows])
    value_padded = jnp.concatenate([padding, value_rows])

    def one_block(block_index):
        first_row = block_index * STRIDE
        query_blk = lax.dynamic_slice_in_dim(query_rows, first_row, STRIDE, 0).astype(jnp.float32)
        key_blk = lax.dynamic_slice_in_dim(key_padded, first_row, 2 * STRIDE, 0).astype(jnp.float32)
        value_blk = lax.dynamic_slice_in_dim(value_padded, first_row, 2 * STRIDE, 0).astype(jnp.float32)
        query_pos = first_row + jnp.arange(STRIDE, dtype=jnp.int32)
        key_pos = first_row - STRIDE + jnp.arange(2 * STRIDE, dtype=jnp.int32)
        distance = query_pos[:, None] - key_pos[None, :]
        allowed = (distance >= 0) & (distance < STRIDE) & (key_pos[None, :] >= 0)
        scores = jnp.einsum('qhe,khe->hqk', query_blk, key_blk, precision=HIGHEST) * SCALE
        rounded, weight_sum = softmax_rows(scores, allowed[None])
        mixed_out = jnp.einsum('hqk,khe->qhe', rounded, value_blk, precision=HIGHEST)
        return mixed_out / jnp.transpose(weight_sum)[:, :, None]
    layer_output = lax.map(one_block, jnp.arange(length // STRIDE, dtype=jnp.int32))
    return layer_output.reshape(query_rows.shape)

def far_attention(query_rows, key_rows, value_rows):
    length, head_count, head_size = query_rows.shape
    grid = (length // STRIDE, STRIDE, head_count, head_size)
    query_cols = query_rows.reshape(grid).astype(jnp.float32)
    key_cols = key_rows.reshape(grid).astype(jnp.float32)
    value_cols = value_rows.reshape(grid).astype(jnp.float32)
    row_order = jnp.arange(length // STRIDE, dtype=jnp.int32)
    allowed = row_order[None, :] <= row_order[:, None]
    scores = jnp.einsum('arhe,brhe->rhab', query_cols, key_cols, precision=HIGHEST) * SCALE
    rounded, weight_sum = softmax_rows(scores, allowed)
    mixed_out = jnp.einsum('rhab,brhe->arhe', rounded, value_cols, precision=HIGHEST)
    mixed_out = mixed_out / jnp.transpose(weight_sum, (2, 0, 1))[..., None]
    return mixed_out.reshape(query_rows.shape)

def stretch_step(ssm_state, block_inputs):
    inner_rows, write_low, read_low, step_rows, decay_rows = block_inputs
    write_rows = write_low.astype(jnp.float32)
    read_rows = read_low.astype(jnp.float32)
    cum_log = jnp.cumsum(decay_rows, axis=1)
    block_size = cum_log.shape[1]
    causal = jnp.arange(block_size)[:, None] >= jnp.arange(block_size)[None, :]
    distance = cum_log[:, :, None] - cum_log[:, None, :]
    decay_matrix = jnp.exp(jnp.where(causal[None], distance, NEGATIVE))
    intersection = jnp.dot(read_low, jnp.transpose(write_low), preferred_element_type=jnp.float32)
    driven = inner_rows * jnp.transpose(step_rows)[:, :, None]
    within = jnp.einsum('hij,jhp->ihp', decay_matrix * intersection[None], driven, precision=HIGHEST)
    from_state = jnp.einsum('in,hpn->ihp', read_rows, ssm_state, precision=HIGHEST)
    from_state = from_state * jnp.transpose(jnp.exp(cum_log))[:, :, None]
    tail_weight = jnp.exp(cum_log[:, -1:] - cum_log) * step_rows
    contrib = jnp.einsum('jhp,jn->hpn', inner_rows * jnp.transpose(tail_weight)[:, :, None], write_rows, precision=HIGHEST)
    new_state = jnp.exp(cum_log[:, -1])[:, None, None] * ssm_state + contrib
    return (new_state, within + from_state)

def reference(queries, key_proj, value_proj, residual, mix_weight, inner_weight, write_weight, read_weight, step_logits, decay_rates, carried_state, carried_valid):

    def one_sequence(sequence_inputs):
        query_in, key_in, value_in, resid_in, logit_rows, carried, valid_flag = sequence_inputs
        length = query_in.shape[0]
        shaped = (length, HEADS // 2, 2, HEAD_DIM)
        query_heads = query_in.reshape(shaped)
        key_heads = key_in.reshape(shaped)
        value_heads = value_in.reshape(shaped)
        near_out = near_attention(query_heads[:, :, 0], key_heads[:, :, 0], value_heads[:, :, 0])
        far_out = far_attention(query_heads[:, :, 1], key_heads[:, :, 1], value_heads[:, :, 1])
        mixed_heads = jnp.stack([near_out, far_out], axis=2).reshape(length, HEADS * HEAD_DIM).astype(jnp.bfloat16)
        branch = jnp.dot(mixed_heads, mix_weight, preferred_element_type=jnp.float32)
        stream = (resid_in.astype(jnp.float32) + branch).astype(jnp.bfloat16)
        stream_f = stream.astype(jnp.float32)
        normed = (stream_f * lax.rsqrt(lax.optimization_barrier(jnp.mean(stream_f * stream_f, axis=-1, keepdims=True)) + EPSILON)).astype(jnp.bfloat16)
        inner = jax.nn.silu(jnp.dot(normed, inner_weight, preferred_element_type=jnp.float32)).astype(jnp.bfloat16)
        write_vec = jnp.dot(normed, write_weight, preferred_element_type=jnp.float32).astype(jnp.bfloat16)
        read_vec = jnp.dot(normed, read_weight, preferred_element_type=jnp.float32).astype(jnp.bfloat16)
        step_size = jax.nn.softplus(logit_rows)
        log_decay = -decay_rates[:, None] * step_size
        block_count = length // STRETCH
        inner_blocks = inner.astype(jnp.float32).reshape(block_count, STRETCH, SSM_HEADS, SSM_DIM)
        write_blocks = write_vec.reshape(block_count, STRETCH, STATE)
        read_blocks = read_vec.reshape(block_count, STRETCH, STATE)
        step_blocks = jnp.transpose(step_size.reshape(SSM_HEADS, block_count, STRETCH), (1, 0, 2))
        decay_blocks = jnp.transpose(log_decay.reshape(SSM_HEADS, block_count, STRETCH), (1, 0, 2))
        initial = jnp.where(valid_flag[:, None, None] != 0, carried, 0.0)
        final_state, outputs = lax.scan(stretch_step, initial, (inner_blocks, write_blocks, read_blocks, step_blocks, decay_blocks))
        scan_out = outputs.reshape(length, SSM_HEADS * SSM_DIM).astype(jnp.bfloat16)
        return (stream, scan_out)
    stream, scan_out = lax.map(one_sequence, (queries, key_proj, value_proj, residual, step_logits, carried_state, carried_valid))
    return (stream, scan_out)
```

```python
import functools

import jax
import jax.numpy as jnp
from jax import lax
from jax.experimental import pallas as pl
from jax.experimental.pallas import tpu as pltpu
from jax.sharding import PartitionSpec as P

MESH = pl.DeviceIdType.MESH
LANES = 128
HALF = 64
STRIDE = 256
STRETCH = 128
SCALE = 0.125
NEGATIVE = -1e30
EPSILON = 1e-05
F32 = jnp.float32
BF16 = jnp.bfloat16


def dot(a, b, contract=((1,), (0,)), precision=None):
    return lax.dot_general(
        a, b, (contract, ((), ())), precision=precision, preferred_element_type=F32
    )


def tile(index):
    return slice(index * LANES, (index + 1) * LANES)


def softplus(x):
    e = jnp.exp(-jnp.abs(x))
    u = 1.0 + e
    low = jnp.where(u == 1.0, e, jnp.log(u) * e / jnp.where(u == 1.0, 1.0, u - 1.0))
    return jnp.maximum(x, 0.0) + low


def layer(
    grp_count,
    tm_count,
    seq_count,
    sub_count,
    q_hbm,
    k_hbm,
    v_hbm,
    res_hbm,
    mix_ref,
    inw_ref,
    ww_ref,
    rw_ref,
    logit_hbm,
    carry_hbm,
    rates_ref,
    valid_ref,
    stream_ref,
    out_ref,
    q_ref,
    k_ref,
    v_ref,
    res_ref,
    logit_ref,
    carry_ref,
    x_out,
    x_in,
    o_out,
    o_in,
    halo_out,
    halo_in,
    mixed,
    mix_all,
    inw_all,
    ww_all,
    rw_all,
    b_out,
    b_in,
    normed,
    inner,
    contrib,
    s_out,
    s_in,
    x_send,
    x_recv,
    o_send,
    o_recv,
    h_send,
    h_recv,
    w_send,
    w_recv,
    f_send,
    f_recv,
    b_send,
    b_recv,
    s_send,
    s_recv,
    l_sem,
):
    me = lax.axis_index("tm")
    my_seq = lax.axis_index("seq")
    my_sub = lax.axis_index("sub")
    my_grp = lax.axis_index("grp")
    pairs = q_ref.shape[2] // LANES
    rows = q_ref.shape[1]
    width = res_ref.shape[2]
    share = STRIDE // tm_count
    heads = rates_ref.shape[0]
    state_pairs = heads // 2
    blocks = rows // STRETCH

    in_rows = inw_ref.shape[0]
    mine = pl.ds(pl.multiple_of(my_seq * in_rows, in_rows), in_rows)
    loads = [
        pltpu.make_async_copy(src, dst, l_sem.at[index])
        for index, (src, dst) in enumerate(
            (
                (k_hbm, k_ref),
                (v_hbm, v_ref),
                (q_hbm, q_ref),
                (logit_hbm, logit_ref),
                (mix_ref, mix_all.at[my_seq]),
                (res_hbm, res_ref),
                (ww_ref, ww_all.at[mine]),
                (rw_ref, rw_all.at[mine]),
                (inw_ref, inw_all.at[mine]),
                (carry_hbm, carry_ref),
            )
        )
    ]
    for load in loads:
        load.start()

    def peers(axis, mine, count):
        return [(d, {axis: lax.rem(mine + d, count)}) for d in range(1, count)]

    tm_peers = peers("tm", me, tm_count)
    seq_peers = peers("seq", my_seq, seq_count)
    sub_peers = peers("sub", my_sub, sub_count)
    barrier = pltpu.get_barrier_semaphore()
    grp_peers = peers("grp", my_grp, grp_count)
    everyone = tm_peers + seq_peers + sub_peers + grp_peers
    for _, peer in everyone:
        pl.semaphore_signal(barrier, inc=1, device_id=peer, device_id_type=MESH)

    for load in loads[:3]:
        load.wait()
    low_half = lax.broadcasted_iota(jnp.int32, (STRIDE, LANES), 1) < HALF

    for which, ref in enumerate((q_ref, k_ref, v_ref)):
        for p in range(pairs):
            first = pltpu.roll(ref[0, :STRIDE, tile(p)].astype(F32), HALF, 1)
            second = ref[0, STRIDE:, tile(p)].astype(F32)
            x_out[:, tile(which * pairs + p)] = jnp.where(low_half, first, second).astype(BF16)
    for p in range(pairs):
        key_tail = k_ref[0, rows - STRIDE :, tile(p)].astype(F32)
        value_tail = pltpu.roll(v_ref[0, rows - STRIDE :, tile(p)].astype(F32), HALF, 1)
        halo_out[:, tile(p)] = jnp.where(low_half, key_tail, value_tail).astype(BF16)

    @pl.when(me == 0)
    def _():
        halo_in[...] = jnp.zeros_like(halo_in)

    pl.semaphore_wait(barrier, len(everyone))

    def remote(src, dst, send, recv, peer):
        return pltpu.make_async_remote_copy(
            src_ref=src,
            dst_ref=dst,
            send_sem=send,
            recv_sem=recv,
            device_id=peer,
            device_id_type=MESH,
        )

    def residues(index):
        return pl.ds(pl.multiple_of(index * share, share), share)

    x_copies = [
        remote(
            x_out.at[residues(peer["tm"])], x_in.at[me], x_send.at[d], x_recv.at[d], peer
        )
        for d, peer in tm_peers
    ]
    for copy in x_copies:
        copy.start()
    ahead = jnp.minimum(me + 1, tm_count - 1)
    halo_copy = remote(halo_out, halo_in, h_send.at[0], h_recv.at[0], {"tm": ahead})

    @pl.when(me < tm_count - 1)
    def _():
        halo_copy.start()

    def region(index, owner):
        if index == 0:
            part = mix_ref.shape[0] // grp_count
            return mix_all.at[owner, pl.ds(pl.multiple_of(my_grp * part, part), part)]
        part = in_rows // grp_count
        start = pl.multiple_of(owner * in_rows + my_grp * part, part)
        return (ww_all, rw_all, inw_all)[index - 1].at[pl.ds(start, part)]

    w_copies, f_copies = [], []
    for index, src in enumerate((mix_ref, ww_ref, rw_ref, inw_ref)):
        part = src.shape[0] // grp_count
        own_part = src.at[pl.ds(pl.multiple_of(my_grp * part, part), part)]
        w_copies.append(
            [
                remote(
                    own_part, region(index, my_seq), w_send.at[index, d], w_recv.at[index, d], peer
                )
                for d, peer in seq_peers
            ]
        )
        f_copies.append([])
        for d, _ in seq_peers:
            place = region(index, lax.rem(my_seq - d + seq_count, seq_count))
            for e, peer in grp_peers:
                f_copies[-1].append(
                    remote(place, place, f_send.at[index, d, e], f_recv.at[index, d, e], peer)
                )
        for copy in w_copies[-1]:
            copy.start()

    def pass_on(index):
        for copy in w_copies[index]:
            copy.wait()
        for copy in f_copies[index]:
            copy.start()

    x_in[me] = x_out[residues(me), :]

    row_at = lax.broadcasted_iota(jnp.int32, (STRIDE, STRIDE), 0)
    col_at = lax.broadcasted_iota(jnp.int32, (STRIDE, STRIDE), 1)
    own_allowed = col_at <= row_at

    def near(block, prev_keys, prev_values, prev_allowed, turned):
        at = slice(block * STRIDE, (block + 1) * STRIDE)
        for p in range(pairs):
            query = jnp.where(low_half, q_ref[0, at, tile(p)].astype(F32) * SCALE, 0.0).astype(BF16)
            own = dot(query, k_ref[0, at, tile(p)], ((1,), (1,)))
            prev = dot(query, prev_keys(p), ((1,), (1,)))
            own = jnp.where(own_allowed, own, NEGATIVE)
            prev = jnp.where(prev_allowed, prev, NEGATIVE)
            top = jnp.maximum(
                jnp.max(own, axis=1, keepdims=True), jnp.max(prev, axis=1, keepdims=True)
            )
            own = jnp.where(own_allowed, jnp.exp(own - top), 0.0)
            prev = jnp.where(prev_allowed, jnp.exp(prev - top), 0.0)
            total = jnp.sum(own, axis=1, keepdims=True) + jnp.sum(prev, axis=1, keepdims=True)
            from_prev = dot(prev.astype(BF16), prev_values(p))
            if turned:
                from_prev = pltpu.roll(from_prev, HALF, 1)
            result = dot(own.astype(BF16), v_ref[0, at, tile(p)]) + from_prev
            mixed[at, tile(p)] = (result / total).astype(BF16)

    near(
        1,
        lambda p: k_ref[0, :STRIDE, tile(p)],
        lambda p: v_ref[0, :STRIDE, tile(p)],
        col_at > row_at,
        False,
    )

    loads[3].wait()
    head_at = lax.broadcasted_iota(jnp.int32, (heads, 1), 0)
    rates = jnp.zeros((heads, 1), F32)
    flags = jnp.zeros((heads, 1), F32)
    for h in range(heads):
        rates = jnp.where(head_at == h, rates_ref[h], rates)
        flags = jnp.where(head_at == h, valid_ref[0, h].astype(F32), flags)
    step = softplus(logit_ref[:, 0, :])
    log_decay = -rates * step
    tri = (
        lax.broadcasted_iota(jnp.int32, (STRETCH, STRETCH), 0)
        <= lax.broadcasted_iota(jnp.int32, (STRETCH, STRETCH), 1)
    ).astype(F32)
    step_rows, cum_rows, cum_cols, grow_cols, tail_cols, block_decay = [], [], [], [], [], []
    for c in range(blocks):
        at = slice(c * STRETCH, (c + 1) * STRETCH)
        cum = dot(log_decay[:, at], tri, precision=lax.Precision.HIGHEST)
        last = cum[:, STRETCH - 1 :]
        tail = jnp.exp(last - cum) * step[:, at]
        step_rows.append(step[:, at])
        cum_rows.append(cum)
        cum_cols.append(jnp.transpose(cum))
        grow_cols.append(jnp.exp(cum_cols[-1]))
        tail_cols.append(jnp.transpose(tail))
        block_decay.append(jnp.exp(last))

    for index in (0, 1, 2):
        pass_on(index)
    for copy in x_copies:
        copy.wait()
    pass_on(3)
    ones = (
        (lax.broadcasted_iota(jnp.int32, (LANES, LANES), 0) < HALF)
        == (lax.broadcasted_iota(jnp.int32, (LANES, LANES), 1) < HALF)
    ).astype(BF16)
    source = lax.broadcasted_iota(jnp.int32, (tm_count, share, LANES), 0)
    upper = lax.broadcasted_iota(jnp.int32, (tm_count, share, LANES), 2) >= HALF
    full = (tm_count * share, LANES)
    cube = (tm_count, share, LANES)

    def lane_sums(product):
        product = product.reshape(full)
        high = product.astype(BF16)
        low = (product - high.astype(F32)).astype(BF16)
        return (dot(high, ones) + dot(low, ones)).reshape(cube)

    o_copies = []
    for p in range(pairs):
        keys = x_in[:, :, tile(pairs + p)].astype(F32)
        values = x_in[:, :, tile(2 * pairs + p)].astype(F32)
        keys_turned = pltpu.roll(keys.reshape(full), HALF, 1).reshape(cube)
        values_turned = pltpu.roll(values.reshape(full), HALF, 1).reshape(cube)

        def far(d, carry, p=p, keys=keys, values=values, kt=keys_turned, vt=values_turned):
            query = x_in[d, :, tile(p)].astype(F32)[None] * SCALE
            allowed = source <= d
            allowed_turned = (source < d) | ((source == d) & upper)
            straight = jnp.where(allowed, lane_sums(keys * query), NEGATIVE)
            turned = jnp.where(allowed_turned, lane_sums(kt * query), NEGATIVE)
            top = jnp.max(jnp.maximum(straight, turned), axis=0, keepdims=True)
            straight = jnp.where(allowed, jnp.exp(straight - top), 0.0)
            turned = jnp.where(allowed_turned, jnp.exp(turned - top), 0.0)
            total = jnp.sum(straight + turned, axis=0)
            result = jnp.sum(
                straight.astype(BF16).astype(F32) * values + turned.astype(BF16).astype(F32) * vt,
                axis=0,
            )
            o_out[d, :, tile(p)] = (result / total).astype(BF16)
            return carry

        lax.fori_loop(0, tm_count, far, 0, unroll=tm_count <= 4)

        for d, peer in tm_peers:
            o_copies.append(
                remote(
                    o_out.at[peer["tm"], :, tile(p)],
                    o_in.at[residues(me), tile(p)],
                    o_send.at[p, d],
                    o_recv.at[p, d],
                    peer,
                )
            )
            o_copies[-1].start()

    o_in[residues(me), :] = o_out[me]

    @pl.when(me > 0)
    def _():
        halo_copy.wait_recv()

    near(
        0,
        lambda p: halo_in[:, tile(p)],
        lambda p: halo_in[:, tile(p)],
        (col_at > row_at) & (me > 0),
        True,
    )
    loads[4].wait()
    for copy in f_copies[0]:
        copy.wait()
    for copy in o_copies:
        copy.wait()

    piece = mix_ref.shape[1]
    b_copies = []
    for a in range(rows // STRIDE):
        at = slice(a * STRIDE, (a + 1) * STRIDE)
        for p in range(pairs):
            far_part = o_in[:, tile(p)].astype(F32)
            if a == 0:
                far_part = pltpu.roll(far_part, HALF, 1)
            mixed[at, tile(p)] = jnp.where(
                low_half, mixed[at, tile(p)].astype(F32), far_part
            ).astype(BF16)
        if piece % LANES == 0:
            for s in range(seq_count):
                b_out[at, s * piece : (s + 1) * piece] = dot(mixed[at, :], mix_all[s]).astype(BF16)
        else:
            total = jnp.zeros((STRIDE, width), F32)
            from_col = lax.broadcasted_iota(jnp.int32, (piece, width), 0)
            to_col = lax.broadcasted_iota(jnp.int32, (piece, width), 1)
            for s in range(seq_count):
                placed = (to_col == from_col + s * piece).astype(BF16)
                weight = dot(mix_all[s], placed).astype(BF16)
                total = total + dot(mixed[at, :], weight)
            b_out[at, :] = total.astype(BF16)
        b_copies.append(
            [
                remote(
                    b_out.at[pl.ds(a * STRIDE, STRIDE)],
                    b_in.at[d - 1, pl.ds(a * STRIDE, STRIDE)],
                    b_send.at[a, d],
                    b_recv.at[a, d],
                    peer,
                )
                for d, peer in sub_peers
            ]
        )
        for copy in b_copies[-1]:
            copy.start()
    for load in loads[5:]:
        load.wait()
    for index in (1, 2, 3):
        for copy in f_copies[index]:
            copy.wait()
    read_vecs, write_vecs = [], []
    for a in range(rows // STRIDE):
        at = slice(a * STRIDE, (a + 1) * STRIDE)
        for copy in b_copies[a]:
            copy.wait()
        branch = b_out[at, :].astype(F32)
        for d, _ in sub_peers:
            branch = branch + b_in[d - 1, at, :].astype(F32)
        stream = (res_ref[0, at, :].astype(F32) + branch).astype(BF16)
        stream_ref[0, at, :] = stream
        wide = stream.astype(F32)
        mean = jnp.sum(wide * wide, axis=1, keepdims=True) * (1.0 / width)
        normed[at, :] = (wide * lax.rsqrt(mean + EPSILON)).astype(BF16)
        write_vec = dot(normed[at, :], ww_all[...]).astype(BF16)
        read_vec = dot(normed[at, :], rw_all[...]).astype(BF16)
        for c in range(STRIDE // STRETCH):
            write_vecs.append(write_vec[c * STRETCH : (c + 1) * STRETCH])
            read_vecs.append(read_vec[c * STRETCH : (c + 1) * STRETCH])
        drive = dot(normed[at, :], inw_all[...])
        inner[at, :] = (drive / (1.0 + jnp.exp(-drive))).astype(BF16)

    low_lane = lax.broadcasted_iota(jnp.int32, (STRETCH, LANES), 1) < HALF
    low_row = lax.broadcasted_iota(jnp.int32, (LANES, LANES), 0) < HALF
    causal = lax.broadcasted_iota(jnp.int32, (STRETCH, STRETCH), 0) >= lax.broadcasted_iota(
        jnp.int32, (STRETCH, STRETCH), 1
    )

    def by_lane(cols, pair):
        return jnp.where(
            low_lane, cols[:, 2 * pair : 2 * pair + 1], cols[:, 2 * pair + 1 : 2 * pair + 2]
        )

    def by_row(entries, pair):
        return jnp.where(
            low_row, entries[2 * pair : 2 * pair + 1], entries[2 * pair + 1 : 2 * pair + 2]
        )

    def s_copy(pair):
        return remote(
            s_out.at[pair], s_in.at[pair], s_send.at[pair], s_recv.at[pair], {"tm": ahead}
        )

    def initial(pair):
        valid = by_row(flags, pair) != 0.0
        return jnp.where(valid, carry_ref[0, tile(pair), :], 0.0)

    def through(state, pair):
        states = []
        for c in range(blocks):
            states.append(state.astype(BF16))
            state = by_row(block_decay[c], pair) * state + contrib[c, tile(pair), :]
        return states, state.astype(BF16)

    for pair in range(state_pairs):
        for c in range(blocks):
            at = slice(c * STRETCH, (c + 1) * STRETCH)
            weighted = inner[at, tile(pair)].astype(F32) * by_lane(tail_cols[c], pair)
            contrib[c, tile(pair), :] = dot(weighted.astype(BF16), write_vecs[c], ((0,), (0,)))

        @pl.when(me == 0)
        def _(pair=pair):
            s_in[pair] = jnp.zeros_like(s_in[pair])
            if tm_count > 1:
                s_out[pair] = through(initial(pair), pair)[1]
                s_copy(pair).start()

    grams = [dot(read_vecs[c], write_vecs[c], ((1,), (1,))) for c in range(blocks)]

    def within_of(pair):
        within = []
        for c in range(blocks):
            at = slice(c * STRETCH, (c + 1) * STRETCH)
            entries = inner[at, tile(pair)]
            parts = []
            for h in (2 * pair, 2 * pair + 1):
                distance = cum_cols[c][:, h : h + 1] - cum_rows[c][h : h + 1, :]
                decay = jnp.exp(jnp.where(causal, distance, NEGATIVE))
                matrix = decay * grams[c] * step_rows[c][h : h + 1, :]
                parts.append(dot(matrix.astype(BF16), entries))
            within.append(jnp.where(low_lane, parts[0], parts[1]))
        return within

    first_device = me == 0
    lead = min(2, state_pairs)
    ready = [within_of(pair) for pair in range(lead)]
    for pair in range(state_pairs):

        @pl.when(me > 0)
        def _(pair=pair):
            s_copy(pair).wait_recv()

        state = jnp.where(first_device, initial(pair), s_in[pair].astype(F32))
        states, final = through(state, pair)

        @pl.when((me > 0) & (me < tm_count - 1))
        def _(pair=pair, final=final):
            s_out[pair] = final
            s_copy(pair).start()

        if pair + lead < state_pairs:
            ready.append(within_of(pair + lead))
        for c in range(blocks):
            at = slice(c * STRETCH, (c + 1) * STRETCH)
            carried = dot(read_vecs[c], states[c], ((1,), (1,))) * by_lane(grow_cols[c], pair)
            out_ref[0, at, tile(pair)] = (ready[pair][c] + carried).astype(BF16)

    @pl.when(me < tm_count - 1)
    def _():
        halo_copy.wait_send()
        for pair in range(state_pairs):
            s_copy(pair).wait_send()


def solution(mesh):
    grp_count, tm_count, seq_count, sub_count = (
        mesh.shape[axis] for axis in ("grp", "tm", "seq", "sub")
    )

    def on_device(
        queries,
        key_proj,
        value_proj,
        residual,
        mix_weight,
        inner_weight,
        write_weight,
        read_weight,
        step_logits,
        decay_rates,
        carried_state,
        carried_valid,
    ):
        rows, columns = queries.shape[1:]
        width = residual.shape[2]
        heads, channels, state_dim = carried_state.shape[1:]
        assert rows == 2 * STRIDE and state_dim == LANES and channels == HALF
        pairs = columns // LANES
        share = STRIDE // tm_count
        inner_columns = inner_weight.shape[1]
        state_pairs = heads // 2
        carried = carried_state.reshape(1, heads * channels, state_dim)
        vmem = pl.BlockSpec(memory_space=pltpu.VMEM)
        smem = pl.BlockSpec(memory_space=pltpu.SMEM)
        anywhere = pl.BlockSpec(memory_space=pl.ANY)
        dma = pltpu.SemaphoreType.DMA
        return pl.pallas_call(
            functools.partial(layer, grp_count, tm_count, seq_count, sub_count),
            out_shape=(
                pltpu.VMEM((1, rows, width), BF16),
                pltpu.VMEM((1, rows, inner_columns), BF16),
            ),
            in_specs=[anywhere] * 10 + [smem] * 2,
            out_specs=(vmem, vmem),
            scratch_shapes=[
                pltpu.VMEM((1, rows, columns), BF16),
                pltpu.VMEM((1, rows, columns), BF16),
                pltpu.VMEM((1, rows, columns), BF16),
                pltpu.VMEM((1, rows, width), BF16),
                pltpu.VMEM((heads, 1, rows), F32),
                pltpu.VMEM((1, heads * channels, state_dim), F32),
                pltpu.VMEM((STRIDE, 3 * columns), BF16),
                pltpu.VMEM((tm_count, share, 3 * columns), BF16),
                pltpu.VMEM((tm_count, share, columns), BF16),
                pltpu.VMEM((STRIDE, columns), BF16),
                pltpu.VMEM((STRIDE, columns), BF16),
                pltpu.VMEM((STRIDE, columns), BF16),
                pltpu.VMEM((rows, columns), BF16),
                pltpu.VMEM((seq_count,) + mix_weight.shape, BF16),
                pltpu.VMEM((width, inner_columns), BF16),
                pltpu.VMEM((width, state_dim), BF16),
                pltpu.VMEM((width, state_dim), BF16),
                pltpu.VMEM((rows, width), BF16),
                pltpu.VMEM((max(sub_count - 1, 1), rows, width), BF16),
                pltpu.VMEM((rows, width), BF16),
                pltpu.VMEM((rows, inner_columns), BF16),
                pltpu.VMEM((rows // STRETCH, heads * channels, state_dim), F32),
                pltpu.VMEM((state_pairs, LANES, state_dim), BF16),
                pltpu.VMEM((state_pairs, LANES, state_dim), BF16),
                dma((tm_count,)),
                dma((tm_count,)),
                dma((pairs, tm_count)),
                dma((pairs, tm_count)),
                dma((1,)),
                dma((1,)),
                dma((4, seq_count)),
                dma((4, seq_count)),
                dma((4, seq_count, grp_count)),
                dma((4, seq_count, grp_count)),
                dma((rows // STRIDE, sub_count)),
                dma((rows // STRIDE, sub_count)),
                dma((state_pairs,)),
                dma((state_pairs,)),
                dma((10,)),
            ],
            compiler_params=pltpu.CompilerParams(
                collective_id=0, has_side_effects=True, vmem_limit_bytes=60 * 1024 * 1024
            ),
        )(
            queries,
            key_proj,
            value_proj,
            residual,
            mix_weight,
            inner_weight,
            write_weight,
            read_weight,
            jnp.transpose(step_logits, (1, 0, 2)),
            carried,
            decay_rates,
            carried_valid,
        )

    in_specs = (
        P(("grp", "seq"), "tm", "sub"),
        P(("grp", "seq"), "tm", "sub"),
        P(("grp", "seq"), "tm", "sub"),
        P(("grp", "seq"), "tm", None),
        P("sub", "seq"),
        P("seq", "sub"),
        P("seq", None),
        P("seq", None),
        P(("grp", "seq"), "sub", "tm"),
        P("sub"),
        P(("grp", "seq"), "sub", None, None),
        P(("grp", "seq"), "sub"),
    )
    out_specs = (P(("grp", "seq"), "tm", None), P(("grp", "seq"), "tm", "sub"))
    return jax.shard_map(
        on_device, mesh=mesh, in_specs=in_specs, out_specs=out_specs, check_vma=False
    )
```

```python
import functools

import jax
import jax.numpy as jnp
from jax import lax
from jax.experimental import pallas as pl
from jax.experimental.pallas import tpu as pltpu
from jax.sharding import PartitionSpec as P

MESH = pl.DeviceIdType.MESH
LANES = 128
HALF = 64
STRIDE = 256
STRETCH = 128
SCALE = 0.125
NEGATIVE = -1e30
EPSILON = 1e-05
F32 = jnp.float32
BF16 = jnp.bfloat16


def dot(a, b, contract=((1,), (0,)), precision=None):
    return lax.dot_general(
        a, b, (contract, ((), ())), precision=precision, preferred_element_type=F32
    )


def tile(index):
    return slice(index * LANES, (index + 1) * LANES)


def softplus(x):
    e = jnp.exp(-jnp.abs(x))
    u = 1.0 + e
    low = jnp.where(u == 1.0, e, jnp.log(u) * e / jnp.where(u == 1.0, 1.0, u - 1.0))
    return jnp.maximum(x, 0.0) + low


def layer(
    grp_count,
    tm_count,
    seq_count,
    sub_count,
    q_hbm,
    k_hbm,
    v_hbm,
    res_hbm,
    mix_ref,
    inw_ref,
    ww_ref,
    rw_ref,
    logit_hbm,
    carry_hbm,
    rates_ref,
    valid_ref,
    stream_ref,
    out_ref,
    q_ref,
    k_ref,
    v_ref,
    res_ref,
    logit_ref,
    carry_ref,
    strided,
    strided_sems,
    o_in,
    halo_out,
    halo_in,
    mixed,
    mix_all,
    inw_all,
    ww_all,
    rw_all,
    b_out,
    b_in,
    normed,
    inner,
    contrib,
    first,
    s_out,
    s_in,
    h_send,
    h_recv,
    w_send,
    w_recv,
    f_send,
    f_recv,
    b_send,
    b_recv,
    s_send,
    s_recv,
    l_sem,
):
    me = lax.axis_index("tm")
    my_seq = lax.axis_index("seq")
    my_sub = lax.axis_index("sub")
    my_grp = lax.axis_index("grp")
    pairs = q_ref.shape[2] // LANES
    rows = q_ref.shape[1]
    width = res_ref.shape[2]
    share = STRIDE // tm_count
    heads = rates_ref.shape[0]
    state_pairs = heads // 2
    blocks = rows // STRETCH

    in_rows = inw_ref.shape[0]
    mine = pl.ds(pl.multiple_of(my_seq * in_rows, in_rows), in_rows)
    loads = [
        pltpu.make_async_copy(src, dst, l_sem.at[index])
        for index, (src, dst) in enumerate(
            (
                (k_hbm, k_ref),
                (v_hbm, v_ref),
                (q_hbm, q_ref),
                (logit_hbm, logit_ref),
                (mix_ref, mix_all.at[my_seq]),
                (res_hbm, res_ref),
                (ww_ref, ww_all.at[mine]),
                (rw_ref, rw_all.at[mine]),
                (inw_ref, inw_all.at[mine]),
                (carry_hbm, carry_ref),
            )
        )
    ]
    for load in loads:
        load.start()

    def peers(axis, mine, count):
        return [(d, {axis: lax.rem(mine + d, count)}) for d in range(1, count)]

    tm_peers = peers("tm", me, tm_count)
    seq_peers = peers("seq", my_seq, seq_count)
    sub_peers = peers("sub", my_sub, sub_count)
    barrier = pltpu.get_barrier_semaphore()
    grp_peers = peers("grp", my_grp, grp_count)
    everyone = tm_peers + seq_peers + sub_peers + grp_peers
    for _, peer in everyone:
        pl.semaphore_signal(barrier, inc=1, device_id=peer, device_id_type=MESH)

    for load in loads[:3]:
        load.wait()
    low_half = lax.broadcasted_iota(jnp.int32, (STRIDE, LANES), 1) < HALF

    hub = tm_count == 4
    if hub:
        q_out, kv_out, q_in, kv_in, part_out, part_in, own_part = strided
        q_send, q_recv, kv_send, kv_recv, p_send, p_recv = strided_sems
    else:
        x_out, x_in, o_out = strided
        x_send, x_recv, o_send, o_recv = strided_sems

    def packed(ref, p):
        first_half = pltpu.roll(ref[0, :STRIDE, tile(p)].astype(F32), HALF, 1)
        second_half = ref[0, STRIDE:, tile(p)].astype(F32)
        return jnp.where(low_half, first_half, second_half).astype(BF16)

    for p in range(pairs):
        if hub:
            q_out[p] = packed(q_ref, p)
            kv_out[p, 0] = packed(k_ref, p)
            kv_out[p, 1] = packed(v_ref, p)
        else:
            for which, ref in enumerate((q_ref, k_ref, v_ref)):
                x_out[:, tile(which * pairs + p)] = packed(ref, p)
    for p in range(pairs):
        key_tail = k_ref[0, rows - STRIDE :, tile(p)].astype(F32)
        value_tail = pltpu.roll(v_ref[0, rows - STRIDE :, tile(p)].astype(F32), HALF, 1)
        halo_out[:, tile(p)] = jnp.where(low_half, key_tail, value_tail).astype(BF16)

    @pl.when(me == 0)
    def _():
        halo_in[...] = jnp.zeros_like(halo_in)

    pl.semaphore_wait(barrier, len(everyone))

    def remote(src, dst, send, recv, peer):
        return pltpu.make_async_remote_copy(
            src_ref=src,
            dst_ref=dst,
            send_sem=send,
            recv_sem=recv,
            device_id=peer,
            device_id_type=MESH,
        )

    def residues(index):
        return pl.ds(pl.multiple_of(index * share, share), share)

    ahead = jnp.minimum(me + 1, tm_count - 1)
    halo_copy = remote(halo_out, halo_in, h_send.at[0], h_recv.at[0], {"tm": ahead})

    if hub:
        odd = lax.rem(me, 2) == 1
        asker = jnp.maximum(me - 2, 0)

        def q_copy(p, slot):
            return remote(
                q_out.at[p], q_in.at[slot, p], q_send.at[p], q_recv.at[slot, p], {"tm": 1}
            )

        def kv_copy(p):
            return remote(kv_out.at[p], kv_in.at[p], kv_send.at[p], kv_recv.at[p], {"tm": ahead})

        def part_copy(p, slot):
            return remote(
                part_out.at[slot, p],
                part_in.at[p],
                p_send.at[slot, p],
                p_recv.at[p],
                {"tm": 2 + slot},
            )

        for p in range(pairs):

            @pl.when(me >= 2)
            def _(p=p):
                q_copy(p, asker).start()

            @pl.when(~odd)
            def _(p=p):
                kv_copy(p).start()
    else:
        x_copies = [
            remote(
                x_out.at[residues(peer["tm"])], x_in.at[me], x_send.at[d], x_recv.at[d], peer
            )
            for d, peer in tm_peers
        ]
        for copy in x_copies:
            copy.start()

    @pl.when(me < tm_count - 1)
    def _():
        halo_copy.start()

    group = 2 * LANES
    groups = inw_ref.shape[1] // group
    sources = [(mix_ref, None), (ww_ref, None), (rw_ref, None)]
    sources += [(inw_ref, slice(g * group, (g + 1) * group)) for g in range(groups)]

    def region(index, owner):
        src, columns = sources[index]
        part = src.shape[0] // grp_count
        if index == 0:
            return mix_all.at[owner, pl.ds(pl.multiple_of(my_grp * part, part), part)]
        start = pl.multiple_of(owner * in_rows + my_grp * part, part)
        if columns is None:
            return (ww_all, rw_all)[index - 1].at[pl.ds(start, part)]
        return inw_all.at[pl.ds(start, part), columns]

    w_copies, f_copies = [], []
    for index, (src, columns) in enumerate(sources):
        part = src.shape[0] // grp_count
        rows_sent = pl.ds(pl.multiple_of(my_grp * part, part), part)
        sent = src.at[rows_sent] if columns is None else src.at[rows_sent, columns]
        w_copies.append(
            [
                remote(
                    sent, region(index, my_seq), w_send.at[index, d], w_recv.at[index, d], peer
                )
                for d, peer in seq_peers
            ]
        )
        f_copies.append([])
        for d, _ in seq_peers:
            place = region(index, lax.rem(my_seq - d + seq_count, seq_count))
            for e, peer in grp_peers:
                f_copies[-1].append(
                    remote(place, place, f_send.at[index, d, e], f_recv.at[index, d, e], peer)
                )
        for copy in w_copies[-1]:
            copy.start()

    def pass_on(index):
        for copy in w_copies[index]:
            copy.wait()
        for copy in f_copies[index]:
            copy.start()

    if not hub:
        x_in[me] = x_out[residues(me), :]

    row_at = lax.broadcasted_iota(jnp.int32, (STRIDE, STRIDE), 0)
    col_at = lax.broadcasted_iota(jnp.int32, (STRIDE, STRIDE), 1)
    own_allowed = col_at <= row_at

    def near(block, prev_keys, prev_values, prev_allowed, turned):
        at = slice(block * STRIDE, (block + 1) * STRIDE)
        for p in range(pairs):
            query = jnp.where(low_half, q_ref[0, at, tile(p)].astype(F32) * SCALE, 0.0).astype(BF16)
            own = dot(query, k_ref[0, at, tile(p)], ((1,), (1,)))
            prev = dot(query, prev_keys(p), ((1,), (1,)))
            own = jnp.where(own_allowed, own, NEGATIVE)
            prev = jnp.where(prev_allowed, prev, NEGATIVE)
            top = jnp.maximum(
                jnp.max(own, axis=1, keepdims=True), jnp.max(prev, axis=1, keepdims=True)
            )
            own = jnp.where(own_allowed, jnp.exp(own - top), 0.0)
            prev = jnp.where(prev_allowed, jnp.exp(prev - top), 0.0)
            total = jnp.sum(own, axis=1, keepdims=True) + jnp.sum(prev, axis=1, keepdims=True)
            from_prev = dot(prev.astype(BF16), prev_values(p))
            if turned:
                from_prev = pltpu.roll(from_prev, HALF, 1)
            result = dot(own.astype(BF16), v_ref[0, at, tile(p)]) + from_prev
            mixed[at, tile(p)] = (result / total).astype(BF16)

    near(
        1,
        lambda p: k_ref[0, :STRIDE, tile(p)],
        lambda p: v_ref[0, :STRIDE, tile(p)],
        col_at > row_at,
        False,
    )

    loads[3].wait()
    head_at = lax.broadcasted_iota(jnp.int32, (heads, 1), 0)
    rates = jnp.zeros((heads, 1), F32)
    flags = jnp.zeros((heads, 1), F32)
    for h in range(heads):
        rates = jnp.where(head_at == h, rates_ref[h], rates)
        flags = jnp.where(head_at == h, valid_ref[0, h].astype(F32), flags)
    step = softplus(logit_ref[:, 0, :])
    log_decay = -rates * step
    tri = (
        lax.broadcasted_iota(jnp.int32, (STRETCH, STRETCH), 0)
        <= lax.broadcasted_iota(jnp.int32, (STRETCH, STRETCH), 1)
    ).astype(F32)
    step_rows, cum_rows, cum_cols, grow_cols, tail_cols, block_decay = [], [], [], [], [], []
    for c in range(blocks):
        at = slice(c * STRETCH, (c + 1) * STRETCH)
        cum = dot(log_decay[:, at], tri, precision=lax.Precision.HIGHEST)
        last = cum[:, STRETCH - 1 :]
        tail = jnp.exp(last - cum) * step[:, at]
        step_rows.append(step[:, at])
        cum_rows.append(cum)
        cum_cols.append(jnp.transpose(cum))
        grow_cols.append(jnp.exp(cum_cols[-1]))
        tail_cols.append(jnp.transpose(tail))
        block_decay.append(jnp.exp(last))

    low_lane = lax.broadcasted_iota(jnp.int32, (STRETCH, LANES), 1) < HALF
    low_row = low_lane[:1]

    def over_lanes(entries, pair):
        return jnp.where(low_row, entries[2 * pair : 2 * pair + 1], entries[2 * pair + 1 : 2 * pair + 2])

    loads[9].wait()
    for pair in range(state_pairs):
        valid = over_lanes(flags, pair) != 0.0
        first[:, tile(pair)] = jnp.where(valid, jnp.transpose(carry_ref[0, tile(pair), :]), 0.0)

    pass_on(0)
    if not hub:
        for index in range(1, len(sources)):
            pass_on(index)
        for copy in x_copies:
            copy.wait()
    ones = (
        (lax.broadcasted_iota(jnp.int32, (LANES, LANES), 0) < HALF)
        == (lax.broadcasted_iota(jnp.int32, (LANES, LANES), 1) < HALF)
    ).astype(BF16)
    if hub:
        upper = ~low_half
        stat_row = lax.broadcasted_iota(jnp.int32, (16, 3 * LANES), 0)
        stat_lane = lax.broadcasted_iota(jnp.int32, (16, 3 * LANES), 1)
        stat_pick = (
            (stat_row < 6) & (stat_lane == (stat_row // 2) * LANES + (stat_row % 2) * HALF)
        ).astype(BF16)
        back_row = lax.broadcasted_iota(jnp.int32, (16, LANES), 0)
        back_low = lax.broadcasted_iota(jnp.int32, (16, LANES), 1) < HALF
        stat_back = ((back_row < 6) & ((back_row % 2 == 0) == back_low)).astype(BF16)

        def lane_sums(product):
            high = product.astype(BF16)
            low = (product - high.astype(F32)).astype(BF16)
            return dot(high, ones) + dot(low, ones)

        def with_turned(ref, p):
            keys, values = ref[p, 0].astype(F32), ref[p, 1].astype(F32)
            return keys, pltpu.roll(keys, HALF, 1), values, pltpu.roll(values, HALF, 1)

        def attend(query, sets, diagonal):
            scores = []
            for index, (keys, keys_turned, _, _) in enumerate(sets):
                straight, turned = lane_sums(keys * query), lane_sums(keys_turned * query)
                if diagonal and index == 0:
                    turned = jnp.where(upper, turned, NEGATIVE)
                scores.append((straight, turned))
            top = functools.reduce(jnp.maximum, [jnp.maximum(*pair) for pair in scores])
            total, result = 0.0, 0.0
            for index, (_, _, values, values_turned) in enumerate(sets):
                straight, turned = (jnp.exp(entry - top) for entry in scores[index])
                if diagonal and index == 0:
                    turned = jnp.where(upper, turned, 0.0)
                total = total + (straight + turned)
                result = result + (
                    straight.astype(BF16).astype(F32) * values
                    + turned.astype(BF16).astype(F32) * values_turned
                )
            return result, total, top

        def keep(p, outcome):
            for index, entry in enumerate(outcome):
                own_part[index, p] = entry

        for p in range(pairs):
            @pl.when(me == 1)
            def _(p=p):
                kv_copy(p).wait_recv()
                sets = (with_turned(kv_out, p), with_turned(kv_in, p))
                for slot in range(2):
                    q_copy(p, slot).wait_recv()
                    query = q_in[slot, p].astype(F32) * SCALE
                    result, total, top = attend(query, sets, False)
                    part_out[slot, p, :STRIDE] = (result / total).astype(BF16)
                    log_sum = top + jnp.log(total)
                    high = log_sum.astype(BF16)
                    left = log_sum - high.astype(F32)
                    middle = left.astype(BF16)
                    low = (left - middle.astype(F32)).astype(BF16)
                    stats = dot(
                        stat_pick, jnp.concatenate([high, middle, low], axis=1), ((1,), (1,))
                    ).astype(BF16)
                    part_out[slot, p, STRIDE : STRIDE + 16] = stats[:, :LANES]
                    part_out[slot, p, STRIDE + 16 :] = stats[:, LANES:]
                    part_copy(p, slot).start()
                keep(p, attend(q_out[p].astype(F32) * SCALE, sets, True))

            @pl.when(me == 3)
            def _(p=p):
                kv_copy(p).wait_recv()
                sets = (with_turned(kv_out, p), with_turned(kv_in, p))
                keep(p, attend(q_out[p].astype(F32) * SCALE, sets, True))

            @pl.when(~odd)
            def _(p=p):
                keep(p, attend(q_out[p].astype(F32) * SCALE, (with_turned(kv_out, p),), True))

            for index in range(p * (len(sources) - 1) // pairs, (p + 1) * (len(sources) - 1) // pairs):
                pass_on(index + 1)
    else:
        source = lax.broadcasted_iota(jnp.int32, (tm_count, share, LANES), 0)
        upper = lax.broadcasted_iota(jnp.int32, (tm_count, share, LANES), 2) >= HALF
        full = (tm_count * share, LANES)
        cube = (tm_count, share, LANES)

        def lane_sums(product):
            product = product.reshape(full)
            high = product.astype(BF16)
            low = (product - high.astype(F32)).astype(BF16)
            return (dot(high, ones) + dot(low, ones)).reshape(cube)

        o_copies = []
        for p in range(pairs):
            keys = x_in[:, :, tile(pairs + p)].astype(F32)
            values = x_in[:, :, tile(2 * pairs + p)].astype(F32)
            keys_turned = pltpu.roll(keys.reshape(full), HALF, 1).reshape(cube)
            values_turned = pltpu.roll(values.reshape(full), HALF, 1).reshape(cube)

            def far(d, carry, p=p, keys=keys, values=values, kt=keys_turned, vt=values_turned):
                query = x_in[d, :, tile(p)].astype(F32)[None] * SCALE
                allowed = source <= d
                allowed_turned = (source < d) | ((source == d) & upper)
                straight = jnp.where(allowed, lane_sums(keys * query), NEGATIVE)
                turned = jnp.where(allowed_turned, lane_sums(kt * query), NEGATIVE)
                top = jnp.max(jnp.maximum(straight, turned), axis=0, keepdims=True)
                straight = jnp.where(allowed, jnp.exp(straight - top), 0.0)
                turned = jnp.where(allowed_turned, jnp.exp(turned - top), 0.0)
                total = jnp.sum(straight + turned, axis=0)
                result = jnp.sum(
                    straight.astype(BF16).astype(F32) * values + turned.astype(BF16).astype(F32) * vt,
                    axis=0,
                )
                o_out[d, :, tile(p)] = (result / total).astype(BF16)
                return carry

            lax.fori_loop(0, tm_count, far, 0, unroll=tm_count <= 4)

            for d, peer in tm_peers:
                o_copies.append(
                    remote(
                        o_out.at[peer["tm"], :, tile(p)],
                        o_in.at[residues(me), tile(p)],
                        o_send.at[p, d],
                        o_recv.at[p, d],
                        peer,
                    )
                )
                o_copies[-1].start()

        o_in[residues(me), :] = o_out[me]

    @pl.when(me > 0)
    def _():
        halo_copy.wait_recv()

    near(
        0,
        lambda p: halo_in[:, tile(p)],
        lambda p: halo_in[:, tile(p)],
        (col_at > row_at) & (me > 0),
        True,
    )
    loads[4].wait()
    for copy in f_copies[0]:
        copy.wait()
    if hub:
        for p in range(pairs):

            @pl.when(me < 2)
            def _(p=p):
                o_in[:, tile(p)] = (own_part[0, p] / own_part[1, p]).astype(BF16)

            @pl.when(me >= 2)
            def _(p=p):
                part_copy(p, 0).wait_recv()
                log_sum = jnp.concatenate(
                    [
                        dot(part_in[p, STRIDE + 16 * half : STRIDE + 16 * (half + 1)], stat_back, ((0,), (0,)))
                        for half in range(2)
                    ],
                    axis=0,
                )
                top = jnp.maximum(own_part[2, p], log_sum)
                own_scale, other_scale = jnp.exp(own_part[2, p] - top), jnp.exp(log_sum - top)
                result = own_part[0, p] * own_scale + part_in[p, :STRIDE].astype(F32) * other_scale
                total = own_part[1, p] * own_scale + other_scale
                o_in[:, tile(p)] = (result / total).astype(BF16)
    else:
        for copy in o_copies:
            copy.wait()

    piece = mix_ref.shape[1]
    b_copies = []
    for a in range(rows // STRIDE):
        at = slice(a * STRIDE, (a + 1) * STRIDE)
        for p in range(pairs):
            far_part = o_in[:, tile(p)].astype(F32)
            if a == 0:
                far_part = pltpu.roll(far_part, HALF, 1)
            mixed[at, tile(p)] = jnp.where(
                low_half, mixed[at, tile(p)].astype(F32), far_part
            ).astype(BF16)
        if piece % LANES == 0:
            for s in range(seq_count):
                b_out[at, s * piece : (s + 1) * piece] = dot(mixed[at, :], mix_all[s]).astype(BF16)
        else:
            total = jnp.zeros((STRIDE, width), F32)
            from_col = lax.broadcasted_iota(jnp.int32, (piece, width), 0)
            to_col = lax.broadcasted_iota(jnp.int32, (piece, width), 1)
            for s in range(seq_count):
                placed = (to_col == from_col + s * piece).astype(BF16)
                weight = dot(mix_all[s], placed).astype(BF16)
                total = total + dot(mixed[at, :], weight)
            b_out[at, :] = total.astype(BF16)
        b_copies.append(
            [
                remote(
                    b_out.at[pl.ds(a * STRIDE, STRIDE)],
                    b_in.at[d - 1, pl.ds(a * STRIDE, STRIDE)],
                    b_send.at[a, d],
                    b_recv.at[a, d],
                    peer,
                )
                for d, peer in sub_peers
            ]
        )
        for copy in b_copies[-1]:
            copy.start()
    for load in loads[5:9]:
        load.wait()
    for index in (1, 2):
        for copy in f_copies[index]:
            copy.wait()
    read_vecs, write_vecs, write_turned = [], [], []
    for a in range(rows // STRIDE):
        at = slice(a * STRIDE, (a + 1) * STRIDE)
        for copy in b_copies[a]:
            copy.wait()
        branch = b_out[at, :].astype(F32)
        for d, _ in sub_peers:
            branch = branch + b_in[d - 1, at, :].astype(F32)
        stream = (res_ref[0, at, :].astype(F32) + branch).astype(BF16)
        stream_ref[0, at, :] = stream
        wide = stream.astype(F32)
        mean = jnp.sum(wide * wide, axis=1, keepdims=True) * (1.0 / width)
        normed[at, :] = (wide * lax.rsqrt(mean + EPSILON)).astype(BF16)
        write_vec = dot(normed[at, :], ww_all[...]).astype(BF16)
        read_vec = dot(normed[at, :], rw_all[...]).astype(BF16)
        for c in range(STRIDE // STRETCH):
            write_vecs.append(write_vec[c * STRETCH : (c + 1) * STRETCH])
            write_turned.append(jnp.transpose(write_vecs[-1].astype(F32)).astype(BF16))
            read_vecs.append(read_vec[c * STRETCH : (c + 1) * STRETCH])
    causal = lax.broadcasted_iota(jnp.int32, (STRETCH, STRETCH), 0) >= lax.broadcasted_iota(
        jnp.int32, (STRETCH, STRETCH), 1
    )

    def by_lane(cols, pair):
        return jnp.where(
            low_lane, cols[:, 2 * pair : 2 * pair + 1], cols[:, 2 * pair + 1 : 2 * pair + 2]
        )

    def s_copy(pair):
        return remote(
            s_out.at[pair], s_in.at[pair], s_send.at[pair], s_recv.at[pair], {"tm": ahead}
        )

    def through(state, pair):
        states = []
        for c in range(blocks):
            states.append(state.astype(BF16))
            state = over_lanes(block_decay[c], pair) * state + contrib[c, :, tile(pair)]
        return states, state.astype(BF16)

    for g in range(groups):
        columns = slice(g * group, (g + 1) * group)
        for copy in f_copies[3 + g]:
            copy.wait()
        for a in range(rows // STRIDE):
            at = slice(a * STRIDE, (a + 1) * STRIDE)
            drive = dot(normed[at, :], inw_all[:, columns])
            inner[at, columns] = (drive / (1.0 + jnp.exp(-drive))).astype(BF16)
        for c in range(blocks):
            at = slice(c * STRETCH, (c + 1) * STRETCH)
            tails = jnp.concatenate([by_lane(tail_cols[c], pair) for pair in (2 * g, 2 * g + 1)], axis=1)
            weighted = (inner[at, columns].astype(F32) * tails).astype(BF16)
            contrib[c, :, columns] = dot(write_turned[c], weighted)
        for pair in (2 * g, 2 * g + 1):

            @pl.when(me == 0)
            def _(pair=pair):
                s_in[pair] = jnp.zeros_like(s_in[pair])
                if tm_count > 1:
                    s_out[pair] = through(first[:, tile(pair)], pair)[1]
                    s_copy(pair).start()

    grams = [dot(read_vecs[c], write_vecs[c], ((1,), (1,))) for c in range(blocks)]

    def within_of(pair):
        within = []
        for c in range(blocks):
            at = slice(c * STRETCH, (c + 1) * STRETCH)
            entries = inner[at, tile(pair)]
            parts = []
            for h in (2 * pair, 2 * pair + 1):
                distance = cum_cols[c][:, h : h + 1] - cum_rows[c][h : h + 1, :]
                decay = jnp.exp(jnp.where(causal, distance, NEGATIVE))
                matrix = decay * grams[c] * step_rows[c][h : h + 1, :]
                parts.append(dot(matrix.astype(BF16), entries))
            within.append(jnp.where(low_lane, parts[0], parts[1]))
        return within

    first_device = me == 0
    lead = min(2, state_pairs)
    ready = [within_of(pair) for pair in range(lead)]
    for pair in range(state_pairs):

        @pl.when(me > 0)
        def _(pair=pair):
            s_copy(pair).wait_recv()

        state = jnp.where(first_device, first[:, tile(pair)], s_in[pair].astype(F32))
        states, final = through(state, pair)

        @pl.when((me > 0) & (me < tm_count - 1))
        def _(pair=pair, final=final):
            s_out[pair] = final
            s_copy(pair).start()

        if pair + lead < state_pairs:
            ready.append(within_of(pair + lead))
        for c in range(blocks):
            at = slice(c * STRETCH, (c + 1) * STRETCH)
            carried = dot(read_vecs[c], states[c]) * by_lane(grow_cols[c], pair)
            out_ref[0, at, tile(pair)] = (ready[pair][c] + carried).astype(BF16)

    @pl.when(me < tm_count - 1)
    def _():
        halo_copy.wait_send()
        for pair in range(state_pairs):
            s_copy(pair).wait_send()

    if hub:
        for p in range(pairs):

            @pl.when(me >= 2)
            def _(p=p):
                q_copy(p, asker).wait_send()

            @pl.when(~odd)
            def _(p=p):
                kv_copy(p).wait_send()

            @pl.when(me == 1)
            def _(p=p):
                for slot in range(2):
                    part_copy(p, slot).wait_send()


def solution(mesh):
    grp_count, tm_count, seq_count, sub_count = (
        mesh.shape[axis] for axis in ("grp", "tm", "seq", "sub")
    )

    def on_device(
        queries,
        key_proj,
        value_proj,
        residual,
        mix_weight,
        inner_weight,
        write_weight,
        read_weight,
        step_logits,
        decay_rates,
        carried_state,
        carried_valid,
    ):
        rows, columns = queries.shape[1:]
        width = residual.shape[2]
        heads, channels, state_dim = carried_state.shape[1:]
        assert rows == 2 * STRIDE and state_dim == LANES and channels == HALF
        pairs = columns // LANES
        share = STRIDE // tm_count
        inner_columns = inner_weight.shape[1]
        state_pairs = heads // 2
        carried = carried_state.reshape(1, heads * channels, state_dim)
        vmem = pl.BlockSpec(memory_space=pltpu.VMEM)
        smem = pl.BlockSpec(memory_space=pltpu.SMEM)
        anywhere = pl.BlockSpec(memory_space=pl.ANY)
        dma = pltpu.SemaphoreType.DMA
        pieces = 3 + inner_columns // (2 * LANES)
        if tm_count == 4:
            strided = (
                pltpu.VMEM((pairs, STRIDE, LANES), BF16),
                pltpu.VMEM((pairs, 2, STRIDE, LANES), BF16),
                pltpu.VMEM((2, pairs, STRIDE, LANES), BF16),
                pltpu.VMEM((pairs, 2, STRIDE, LANES), BF16),
                pltpu.VMEM((2, pairs, STRIDE + 32, LANES), BF16),
                pltpu.VMEM((pairs, STRIDE + 32, LANES), BF16),
                pltpu.VMEM((3, pairs, STRIDE, LANES), F32),
            )
            strided_sems = tuple(
                dma(extent)
                for extent in ((pairs,), (2, pairs), (pairs,), (pairs,), (2, pairs), (pairs,))
            )
        else:
            strided = (
                pltpu.VMEM((STRIDE, 3 * columns), BF16),
                pltpu.VMEM((tm_count, share, 3 * columns), BF16),
                pltpu.VMEM((tm_count, share, columns), BF16),
            )
            strided_sems = tuple(
                dma(extent)
                for extent in ((tm_count,), (tm_count,), (pairs, tm_count), (pairs, tm_count))
            )
        return pl.pallas_call(
            functools.partial(layer, grp_count, tm_count, seq_count, sub_count),
            out_shape=(
                pltpu.VMEM((1, rows, width), BF16),
                pltpu.VMEM((1, rows, inner_columns), BF16),
            ),
            in_specs=[anywhere] * 10 + [smem] * 2,
            out_specs=(vmem, vmem),
            scratch_shapes=[
                pltpu.VMEM((1, rows, columns), BF16),
                pltpu.VMEM((1, rows, columns), BF16),
                pltpu.VMEM((1, rows, columns), BF16),
                pltpu.VMEM((1, rows, width), BF16),
                pltpu.VMEM((heads, 1, rows), F32),
                pltpu.VMEM((1, heads * channels, state_dim), F32),
                strided,
                strided_sems,
                pltpu.VMEM((STRIDE, columns), BF16),
                pltpu.VMEM((STRIDE, columns), BF16),
                pltpu.VMEM((STRIDE, columns), BF16),
                pltpu.VMEM((rows, columns), BF16),
                pltpu.VMEM((seq_count,) + mix_weight.shape, BF16),
                pltpu.VMEM((width, inner_columns), BF16),
                pltpu.VMEM((width, state_dim), BF16),
                pltpu.VMEM((width, state_dim), BF16),
                pltpu.VMEM((rows, width), BF16),
                pltpu.VMEM((max(sub_count - 1, 1), rows, width), BF16),
                pltpu.VMEM((rows, width), BF16),
                pltpu.VMEM((rows, inner_columns), BF16),
                pltpu.VMEM((rows // STRETCH, state_dim, heads * channels), F32),
                pltpu.VMEM((state_dim, heads * channels), F32),
                pltpu.VMEM((state_pairs, LANES, state_dim), BF16),
                pltpu.VMEM((state_pairs, LANES, state_dim), BF16),
                dma((1,)),
                dma((1,)),
                dma((pieces, seq_count)),
                dma((pieces, seq_count)),
                dma((pieces, seq_count, grp_count)),
                dma((pieces, seq_count, grp_count)),
                dma((rows // STRIDE, sub_count)),
                dma((rows // STRIDE, sub_count)),
                dma((state_pairs,)),
                dma((state_pairs,)),
                dma((10,)),
            ],
            compiler_params=pltpu.CompilerParams(
                collective_id=0, has_side_effects=True, vmem_limit_bytes=60 * 1024 * 1024
            ),
        )(
            queries,
            key_proj,
            value_proj,
            residual,
            mix_weight,
            inner_weight,
            write_weight,
            read_weight,
            jnp.transpose(step_logits, (1, 0, 2)),
            carried,
            decay_rates,
            carried_valid,
        )

    in_specs = (
        P(("grp", "seq"), "tm", "sub"),
        P(("grp", "seq"), "tm", "sub"),
        P(("grp", "seq"), "tm", "sub"),
        P(("grp", "seq"), "tm", None),
        P("sub", "seq"),
        P("seq", "sub"),
        P("seq", None),
        P("seq", None),
        P(("grp", "seq"), "sub", "tm"),
        P("sub"),
        P(("grp", "seq"), "sub", None, None),
        P(("grp", "seq"), "sub"),
    )
    out_specs = (P(("grp", "seq"), "tm", None), P(("grp", "seq"), "tm", "sub"))
    return jax.shard_map(
        on_device, mesh=mesh, in_specs=in_specs, out_specs=out_specs, check_vma=False
    )
```

```python
import functools

import jax
import jax.numpy as jnp
from jax import lax
from jax.experimental import pallas as pl
from jax.experimental.pallas import tpu as pltpu
from jax.sharding import PartitionSpec as P

MESH = pl.DeviceIdType.MESH
LANES = 128
HALF = 64
STRIDE = 256
STRETCH = 128
SCALE = 0.125
NEGATIVE = -1e30
EPSILON = 1e-05
F32 = jnp.float32
BF16 = jnp.bfloat16


def dot(a, b, contract=((1,), (0,)), precision=None):
    return lax.dot_general(
        a, b, (contract, ((), ())), precision=precision, preferred_element_type=F32
    )


def tile(index):
    return slice(index * LANES, (index + 1) * LANES)


def softplus(x):
    e = jnp.exp(-jnp.abs(x))
    u = 1.0 + e
    low = jnp.where(u == 1.0, e, jnp.log(u) * e / jnp.where(u == 1.0, 1.0, u - 1.0))
    return jnp.maximum(x, 0.0) + low


def layer(
    grp_count,
    tm_count,
    seq_count,
    sub_count,
    q_hbm,
    k_hbm,
    v_hbm,
    res_hbm,
    mix_ref,
    inw_ref,
    ww_ref,
    rw_ref,
    logit_hbm,
    carry_hbm,
    rates_ref,
    valid_ref,
    stream_ref,
    out_ref,
    q_ref,
    k_ref,
    v_ref,
    res_ref,
    logit_ref,
    carry_ref,
    strided,
    strided_sems,
    o_in,
    halo_out,
    halo_in,
    mixed,
    mix_all,
    inw_all,
    ww_all,
    rw_all,
    b_out,
    b_in,
    normed,
    inner,
    contrib,
    decays,
    states,
    first,
    s_out,
    s_in,
    h_send,
    h_recv,
    w_send,
    w_recv,
    f_send,
    f_recv,
    b_send,
    b_recv,
    s_send,
    s_recv,
    l_sem,
):
    me = lax.axis_index("tm")
    my_seq = lax.axis_index("seq")
    my_sub = lax.axis_index("sub")
    my_grp = lax.axis_index("grp")
    pairs = q_ref.shape[2] // LANES
    rows = q_ref.shape[1]
    width = res_ref.shape[2]
    share = STRIDE // tm_count
    heads = rates_ref.shape[0]
    state_pairs = heads // 2
    blocks = rows // STRETCH

    in_rows = inw_ref.shape[0]
    mine = pl.ds(pl.multiple_of(my_seq * in_rows, in_rows), in_rows)

    def peers(axis, mine, count):
        return [(d, {axis: lax.rem(mine + d, count)}) for d in range(1, count)]

    tm_peers = peers("tm", me, tm_count)
    seq_peers = peers("seq", my_seq, seq_count)
    sub_peers = peers("sub", my_sub, sub_count)
    grp_peers = peers("grp", my_grp, grp_count)
    barrier = pltpu.get_barrier_semaphore()
    hub = tm_count == 4
    greeted = seq_peers + sub_peers + grp_peers + ([] if hub else tm_peers)
    for _, peer in greeted:
        pl.semaphore_signal(barrier, inc=1, device_id=peer, device_id_type=MESH)
    arrivals = len(greeted)
    if hub:
        arrivals = arrivals + jnp.where(me == 0, 1, jnp.where(me == 1, 3, 2))
        for t in range(tm_count):
            apart = (me == t) | ((me == 0) & (t >= 2)) | ((me >= 2) & (t == 0))

            @pl.when(~apart)
            def _(t=t):
                pl.semaphore_signal(barrier, inc=1, device_id={"tm": t}, device_id_type=MESH)

    group = 2 * LANES
    groups = inw_ref.shape[1] // group
    moves = [("q", q_hbm, q_ref), ("k", k_hbm, k_ref), ("v", v_hbm, v_ref)]
    moves += [("mix", mix_ref, mix_all.at[my_seq])]
    moves += [("ww", ww_ref, ww_all.at[mine]), ("rw", rw_ref, rw_all.at[mine])]
    moves += [
        ("inw%d" % g, inw_ref.at[:, g * group : (g + 1) * group], inw_all.at[g, mine])
        for g in range(groups)
    ]
    moves += [("logit", logit_hbm, logit_ref), ("res", res_hbm, res_ref)]
    moves += [("carry", carry_hbm, carry_ref)]
    loads = {
        name: pltpu.make_async_copy(src, dst, l_sem.at[index])
        for index, (name, src, dst) in enumerate(moves)
    }
    for load in loads.values():
        load.start()
    loads["q"].wait()
    if not hub:
        loads["k"].wait()
        loads["v"].wait()
    low_half = lax.broadcasted_iota(jnp.int32, (STRIDE, LANES), 1) < HALF

    if hub:
        q_out, kv_out, q_in, kv_in, part_out, part_in, own_part = strided
        q_send, q_recv, kv_send, kv_recv, p_send, p_recv = strided_sems
    else:
        x_out, x_in, o_out = strided
        x_send, x_recv, o_send, o_recv = strided_sems

    def packed(ref, p):
        first_half = pltpu.roll(ref[0, :STRIDE, tile(p)].astype(F32), HALF, 1)
        second_half = ref[0, STRIDE:, tile(p)].astype(F32)
        return jnp.where(low_half, first_half, second_half).astype(BF16)

    for p in range(pairs):
        if hub:
            q_out[p] = packed(q_ref, p)
        else:
            for which, ref in enumerate((q_ref, k_ref, v_ref)):
                x_out[:, tile(which * pairs + p)] = packed(ref, p)

    def remote(src, dst, send, recv, peer):
        return pltpu.make_async_remote_copy(
            src_ref=src,
            dst_ref=dst,
            send_sem=send,
            recv_sem=recv,
            device_id=peer,
            device_id_type=MESH,
        )

    pl.semaphore_wait(barrier, arrivals)
    ahead = jnp.minimum(me + 1, tm_count - 1)
    if hub:
        asker = jnp.maximum(me - 2, 0)

        def q_copy(p, slot, to=1):
            sent = q_send.at[p] if to == 1 else q_send.at[pairs + p]
            return remote(q_out.at[p], q_in.at[slot, p], sent, q_recv.at[slot, p], {"tm": to})

        def kv_copy(p):
            return remote(kv_out.at[p], kv_in.at[p], kv_send.at[p], kv_recv.at[p], {"tm": 1})

        def part_copy(p, slot, to, place):
            return remote(
                part_out.at[slot, p],
                part_in.at[place, p],
                p_send.at[slot, p],
                p_recv.at[place, p],
                {"tm": to},
            )

        for p in range(pairs):

            @pl.when(me >= 2)
            def _(p=p):
                q_copy(p, asker).start()

        loads["k"].wait()
        loads["v"].wait()
        for p in range(pairs):
            kv_out[p, 0] = packed(k_ref, p)
            kv_out[p, 1] = packed(v_ref, p)

            @pl.when(me == 0)
            def _(p=p):
                kv_copy(p).start()

    for p in range(pairs):
        key_tail = k_ref[0, rows - STRIDE :, tile(p)].astype(F32)
        value_tail = pltpu.roll(v_ref[0, rows - STRIDE :, tile(p)].astype(F32), HALF, 1)
        halo_out[:, tile(p)] = jnp.where(low_half, key_tail, value_tail).astype(BF16)

    @pl.when(me == 0)
    def _():
        halo_in[...] = jnp.zeros_like(halo_in)

    def residues(index):
        return pl.ds(pl.multiple_of(index * share, share), share)

    halo_copy = remote(halo_out, halo_in, h_send.at[0], h_recv.at[0], {"tm": ahead})
    if not hub:
        x_copies = [
            remote(
                x_out.at[residues(peer["tm"])], x_in.at[me], x_send.at[d], x_recv.at[d], peer
            )
            for d, peer in tm_peers
        ]
        for copy in x_copies:
            copy.start()

    @pl.when(me < tm_count - 1)
    def _():
        halo_copy.start()

    if hub:
        for p in range(pairs):

            @pl.when(me == 3)
            def _(p=p):
                q_copy(p, 0, 2).start()

    pieces = ["mix", "ww", "rw"] + ["inw%d" % g for g in range(groups)]

    def region(index, owner):
        if index == 0:
            part = mix_ref.shape[0] // grp_count
            return mix_all.at[owner, pl.ds(pl.multiple_of(my_grp * part, part), part)]
        part = in_rows // grp_count
        at = pl.ds(pl.multiple_of(owner * in_rows + my_grp * part, part), part)
        return (ww_all, rw_all)[index - 1].at[at] if index < 3 else inw_all.at[index - 3, at]

    w_copies, f_copies = [], []
    for index, name in enumerate(pieces):
        loads[name].wait()
        own = region(index, my_seq)
        w_copies.append(
            [
                remote(own, own, w_send.at[index, d], w_recv.at[index, d], peer)
                for d, peer in seq_peers
            ]
        )
        f_copies.append([])
        for d, _ in seq_peers:
            place = region(index, lax.rem(my_seq - d + seq_count, seq_count))
            for e, peer in grp_peers:
                f_copies[-1].append(
                    remote(place, place, f_send.at[index, d, e], f_recv.at[index, d, e], peer)
                )
        for copy in w_copies[-1]:
            copy.start()

    def pass_on(index):
        for copy in w_copies[index]:
            copy.wait()
        for copy in f_copies[index]:
            copy.start()

    if not hub:
        x_in[me] = x_out[residues(me), :]

    row_at = lax.broadcasted_iota(jnp.int32, (STRIDE, STRIDE), 0)
    col_at = lax.broadcasted_iota(jnp.int32, (STRIDE, STRIDE), 1)
    own_allowed = col_at <= row_at

    def near(block, prev_keys, prev_values, prev_allowed, turned):
        at = slice(block * STRIDE, (block + 1) * STRIDE)
        for p in range(pairs):
            query = jnp.where(low_half, q_ref[0, at, tile(p)].astype(F32) * SCALE, 0.0).astype(BF16)
            own = dot(query, k_ref[0, at, tile(p)], ((1,), (1,)))
            prev = dot(query, prev_keys(p), ((1,), (1,)))
            own = jnp.where(own_allowed, own, NEGATIVE)
            prev = jnp.where(prev_allowed, prev, NEGATIVE)
            top = jnp.maximum(
                jnp.max(own, axis=1, keepdims=True), jnp.max(prev, axis=1, keepdims=True)
            )
            own = jnp.where(own_allowed, jnp.exp(own - top), 0.0)
            prev = jnp.where(prev_allowed, jnp.exp(prev - top), 0.0)
            total = jnp.sum(own, axis=1, keepdims=True) + jnp.sum(prev, axis=1, keepdims=True)
            from_prev = dot(prev.astype(BF16), prev_values(p))
            if turned:
                from_prev = pltpu.roll(from_prev, HALF, 1)
            result = dot(own.astype(BF16), v_ref[0, at, tile(p)]) + from_prev
            mixed[at, tile(p)] = (result / total).astype(BF16)

    near(
        1,
        lambda p: k_ref[0, :STRIDE, tile(p)],
        lambda p: v_ref[0, :STRIDE, tile(p)],
        col_at > row_at,
        False,
    )

    loads["logit"].wait()
    head_at = lax.broadcasted_iota(jnp.int32, (heads, 1), 0)
    rates = jnp.zeros((heads, 1), F32)
    flags = jnp.zeros((heads, 1), F32)
    for h in range(heads):
        rates = jnp.where(head_at == h, rates_ref[h], rates)
        flags = jnp.where(head_at == h, valid_ref[0, h].astype(F32), flags)
    step = softplus(logit_ref[:, 0, :])
    log_decay = -rates * step
    tri = (
        lax.broadcasted_iota(jnp.int32, (STRETCH, STRETCH), 0)
        <= lax.broadcasted_iota(jnp.int32, (STRETCH, STRETCH), 1)
    ).astype(F32)
    step_rows, cum_rows, cum_cols, grow_cols, tail_cols, block_decay = [], [], [], [], [], []
    for c in range(blocks):
        at = slice(c * STRETCH, (c + 1) * STRETCH)
        cum = dot(log_decay[:, at], tri, precision=lax.Precision.HIGHEST)
        last = cum[:, STRETCH - 1 :]
        tail = jnp.exp(last - cum) * step[:, at]
        step_rows.append(step[:, at])
        cum_rows.append(cum)
        cum_cols.append(jnp.transpose(cum))
        grow_cols.append(jnp.exp(cum_cols[-1]))
        tail_cols.append(jnp.transpose(tail))
        block_decay.append(jnp.exp(last))

    low_lane = lax.broadcasted_iota(jnp.int32, (STRETCH, LANES), 1) < HALF
    low_row = low_lane[:1]

    def over_lanes(entries, pair):
        return jnp.where(low_row, entries[2 * pair : 2 * pair + 1], entries[2 * pair + 1 : 2 * pair + 2])

    loads["carry"].wait()
    for pair in range(state_pairs):
        valid = over_lanes(flags, pair) != 0.0
        first[:, tile(pair)] = jnp.where(valid, jnp.transpose(carry_ref[0, tile(pair), :]), 0.0)

    causal = lax.broadcasted_iota(jnp.int32, (STRETCH, STRETCH), 0) >= lax.broadcasted_iota(
        jnp.int32, (STRETCH, STRETCH), 1
    )
    for c in range(blocks):
        for h in range(heads):
            distance = cum_cols[c][:, h : h + 1] - cum_rows[c][h : h + 1, :]
            decay = jnp.exp(jnp.where(causal, distance, NEGATIVE))
            decays[c, h] = decay * step_rows[c][h : h + 1, :]

    pass_on(0)
    if not hub:
        for index in range(1, len(pieces)):
            pass_on(index)
        for copy in x_copies:
            copy.wait()
    ones = (
        (lax.broadcasted_iota(jnp.int32, (LANES, LANES), 0) < HALF)
        == (lax.broadcasted_iota(jnp.int32, (LANES, LANES), 1) < HALF)
    ).astype(BF16)
    if hub:
        upper = ~low_half
        stat_row = lax.broadcasted_iota(jnp.int32, (16, 3 * LANES), 0)
        stat_lane = lax.broadcasted_iota(jnp.int32, (16, 3 * LANES), 1)
        stat_pick = (
            (stat_row < 6) & (stat_lane == (stat_row // 2) * LANES + (stat_row % 2) * HALF)
        ).astype(BF16)
        back_row = lax.broadcasted_iota(jnp.int32, (16, LANES), 0)
        back_low = lax.broadcasted_iota(jnp.int32, (16, LANES), 1) < HALF
        stat_back = ((back_row < 6) & ((back_row % 2 == 0) == back_low)).astype(BF16)

        def lane_sums(product):
            high = product.astype(BF16)
            low = (product - high.astype(F32)).astype(BF16)
            return dot(high, ones) + dot(low, ones)

        def with_turned(ref, p):
            keys, values = ref[p, 0].astype(F32), ref[p, 1].astype(F32)
            return keys, pltpu.roll(keys, HALF, 1), values, pltpu.roll(values, HALF, 1)

        def attend(query, sets, diagonal):
            scores = []
            for index, (keys, keys_turned, _, _) in enumerate(sets):
                straight, turned = lane_sums(keys * query), lane_sums(keys_turned * query)
                if diagonal and index == 0:
                    turned = jnp.where(upper, turned, NEGATIVE)
                scores.append((straight, turned))
            top = functools.reduce(jnp.maximum, [jnp.maximum(*pair) for pair in scores])
            total, result = 0.0, 0.0
            for index, (_, _, values, values_turned) in enumerate(sets):
                straight, turned = (jnp.exp(entry - top) for entry in scores[index])
                if diagonal and index == 0:
                    turned = jnp.where(upper, turned, 0.0)
                total = total + (straight + turned)
                result = result + (
                    straight.astype(BF16).astype(F32) * values
                    + turned.astype(BF16).astype(F32) * values_turned
                )
            return result, total, top

        def keep(p, sets):
            outcome = attend(q_out[p].astype(F32) * SCALE, sets, True)
            for index, entry in enumerate(outcome):
                own_part[index, p] = entry

        def serve(p, slot, sets, to, place):
            q_copy(p, slot).wait_recv()
            result, total, top = attend(q_in[slot, p].astype(F32) * SCALE, sets, False)
            part_out[slot, p, :STRIDE] = (result / total).astype(BF16)
            log_sum = top + jnp.log(total)
            high = log_sum.astype(BF16)
            left = log_sum - high.astype(F32)
            middle = left.astype(BF16)
            low = (left - middle.astype(F32)).astype(BF16)
            stats = dot(
                stat_pick, jnp.concatenate([high, middle, low], axis=1), ((1,), (1,))
            ).astype(BF16)
            part_out[slot, p, STRIDE : STRIDE + 16] = stats[:, :LANES]
            part_out[slot, p, STRIDE + 16 :] = stats[:, LANES:]
            part_copy(p, slot, to, place).start()

        pass_at = {0: (1, 2), 1: (3,)}
        for p in range(pairs):

            @pl.when(me == 1)
            def _(p=p):
                kv_copy(p).wait_recv()
                sets = (with_turned(kv_out, p), with_turned(kv_in, p))
                for slot in range(2):
                    serve(p, slot, sets, 2 + slot, 0)
                keep(p, sets)

            @pl.when(me == 2)
            def _(p=p):
                sets = (with_turned(kv_out, p),)
                serve(p, 0, sets, 3, 1)
                keep(p, sets)

            @pl.when((me == 0) | (me == 3))
            def _(p=p):
                keep(p, (with_turned(kv_out, p),))

            for index in pass_at.get(p, ()):
                pass_on(index)
    else:
        source = lax.broadcasted_iota(jnp.int32, (tm_count, share, LANES), 0)
        upper = lax.broadcasted_iota(jnp.int32, (tm_count, share, LANES), 2) >= HALF
        full = (tm_count * share, LANES)
        cube = (tm_count, share, LANES)

        def lane_sums(product):
            product = product.reshape(full)
            high = product.astype(BF16)
            low = (product - high.astype(F32)).astype(BF16)
            return (dot(high, ones) + dot(low, ones)).reshape(cube)

        o_copies = []
        for p in range(pairs):
            keys = x_in[:, :, tile(pairs + p)].astype(F32)
            values = x_in[:, :, tile(2 * pairs + p)].astype(F32)
            keys_turned = pltpu.roll(keys.reshape(full), HALF, 1).reshape(cube)
            values_turned = pltpu.roll(values.reshape(full), HALF, 1).reshape(cube)

            def far(d, carry, p=p, keys=keys, values=values, kt=keys_turned, vt=values_turned):
                query = x_in[d, :, tile(p)].astype(F32)[None] * SCALE
                allowed = source <= d
                allowed_turned = (source < d) | ((source == d) & upper)
                straight = jnp.where(allowed, lane_sums(keys * query), NEGATIVE)
                turned = jnp.where(allowed_turned, lane_sums(kt * query), NEGATIVE)
                top = jnp.max(jnp.maximum(straight, turned), axis=0, keepdims=True)
                straight = jnp.where(allowed, jnp.exp(straight - top), 0.0)
                turned = jnp.where(allowed_turned, jnp.exp(turned - top), 0.0)
                total = jnp.sum(straight + turned, axis=0)
                result = jnp.sum(
                    straight.astype(BF16).astype(F32) * values + turned.astype(BF16).astype(F32) * vt,
                    axis=0,
                )
                o_out[d, :, tile(p)] = (result / total).astype(BF16)
                return carry

            lax.fori_loop(0, tm_count, far, 0, unroll=tm_count <= 4)

            for d, peer in tm_peers:
                o_copies.append(
                    remote(
                        o_out.at[peer["tm"], :, tile(p)],
                        o_in.at[residues(me), tile(p)],
                        o_send.at[p, d],
                        o_recv.at[p, d],
                        peer,
                    )
                )
                o_copies[-1].start()

        o_in[residues(me), :] = o_out[me]

    @pl.when(me > 0)
    def _():
        halo_copy.wait_recv()

    near(
        0,
        lambda p: halo_in[:, tile(p)],
        lambda p: halo_in[:, tile(p)],
        (col_at > row_at) & (me > 0),
        True,
    )
    if hub:
        for index in range(4, len(pieces) - 1):
            pass_on(index)
        for p in range(pairs):
            if p == pairs - 1:
                pass_on(len(pieces) - 1)

            @pl.when(me < 2)
            def _(p=p):
                o_in[:, tile(p)] = (own_part[0, p] / own_part[1, p]).astype(BF16)

            for count, condition in ((1, me == 2), (2, me == 3)):

                @pl.when(condition)
                def _(p=p, count=count):
                    log_sums = []
                    for place in range(count):
                        part_copy(p, 0, 2, place).wait_recv()
                        halves = [
                            part_in[place, p, STRIDE + 16 * half : STRIDE + 16 * (half + 1)]
                            for half in range(2)
                        ]
                        log_sums.append(
                            jnp.concatenate(
                                [dot(half, stat_back, ((0,), (0,))) for half in halves], axis=0
                            )
                        )
                    top = functools.reduce(jnp.maximum, log_sums, own_part[2, p])
                    scale = jnp.exp(own_part[2, p] - top)
                    result, total = own_part[0, p] * scale, own_part[1, p] * scale
                    for place in range(count):
                        scale = jnp.exp(log_sums[place] - top)
                        result = result + part_in[place, p, :STRIDE].astype(F32) * scale
                        total = total + scale
                    o_in[:, tile(p)] = (result / total).astype(BF16)
    else:
        for copy in o_copies:
            copy.wait()
    for copy in f_copies[0]:
        copy.wait()

    piece = mix_ref.shape[1]
    b_copies = []
    for a in range(rows // STRIDE):
        at = slice(a * STRIDE, (a + 1) * STRIDE)
        for p in range(pairs):
            far_part = o_in[:, tile(p)].astype(F32)
            if a == 0:
                far_part = pltpu.roll(far_part, HALF, 1)
            mixed[at, tile(p)] = jnp.where(
                low_half, mixed[at, tile(p)].astype(F32), far_part
            ).astype(BF16)
        if piece % LANES == 0:
            for s in range(seq_count):
                b_out[at, s * piece : (s + 1) * piece] = dot(mixed[at, :], mix_all[s]).astype(BF16)
        else:
            total = jnp.zeros((STRIDE, width), F32)
            from_col = lax.broadcasted_iota(jnp.int32, (piece, width), 0)
            to_col = lax.broadcasted_iota(jnp.int32, (piece, width), 1)
            for s in range(seq_count):
                placed = (to_col == from_col + s * piece).astype(BF16)
                weight = dot(mix_all[s], placed).astype(BF16)
                total = total + dot(mixed[at, :], weight)
            b_out[at, :] = total.astype(BF16)
        b_copies.append(
            [
                remote(
                    b_out.at[pl.ds(a * STRIDE, STRIDE)],
                    b_in.at[d - 1, pl.ds(a * STRIDE, STRIDE)],
                    b_send.at[a, d],
                    b_recv.at[a, d],
                    peer,
                )
                for d, peer in sub_peers
            ]
        )
        for copy in b_copies[-1]:
            copy.start()
    loads["res"].wait()
    for index in (1, 2):
        for copy in f_copies[index]:
            copy.wait()
    read_vecs, write_vecs, write_turned = [], [], []
    for a in range(rows // STRIDE):
        at = slice(a * STRIDE, (a + 1) * STRIDE)
        for copy in b_copies[a]:
            copy.wait()
        branch = b_out[at, :].astype(F32)
        for d, _ in sub_peers:
            branch = branch + b_in[d - 1, at, :].astype(F32)
        stream = (res_ref[0, at, :].astype(F32) + branch).astype(BF16)
        stream_ref[0, at, :] = stream
        wide = stream.astype(F32)
        mean = jnp.sum(wide * wide, axis=1, keepdims=True) * (1.0 / width)
        normed[at, :] = (wide * lax.rsqrt(mean + EPSILON)).astype(BF16)
        write_vec = dot(normed[at, :], ww_all[...]).astype(BF16)
        read_vec = dot(normed[at, :], rw_all[...]).astype(BF16)
        for c in range(STRIDE // STRETCH):
            write_vecs.append(write_vec[c * STRETCH : (c + 1) * STRETCH])
            write_turned.append(jnp.transpose(write_vecs[-1].astype(F32)).astype(BF16))
            read_vecs.append(read_vec[c * STRETCH : (c + 1) * STRETCH])
    def by_lane(cols, pair):
        return jnp.where(
            low_lane, cols[:, 2 * pair : 2 * pair + 1], cols[:, 2 * pair + 1 : 2 * pair + 2]
        )

    def s_copy(pair):
        return remote(
            s_out.at[pair], s_in.at[pair], s_send.at[pair], s_recv.at[pair], {"tm": ahead}
        )

    def take_state(pair):
        @pl.when(me > 0)
        def _():
            s_copy(pair).wait_recv()

        @pl.when(me == 0)
        def _():
            s_in[pair] = first[:, tile(pair)].astype(BF16)

        state = jnp.where(me == 0, first[:, tile(pair)], s_in[pair].astype(F32))
        for c in range(blocks):
            states[c, :, tile(pair)] = state.astype(BF16)
            state = over_lanes(block_decay[c], pair) * state + contrib[c, :, tile(pair)]
        s_out[pair] = state.astype(BF16)

    for g in range(groups):
        columns = slice(g * group, (g + 1) * group)
        for copy in f_copies[3 + g]:
            copy.wait()
        for a in range(rows // STRIDE):
            at = slice(a * STRIDE, (a + 1) * STRIDE)
            drive = dot(normed[at, :], inw_all[g])
            inner[at, columns] = (drive / (1.0 + jnp.exp(-drive))).astype(BF16)
        for c in range(blocks):
            at = slice(c * STRETCH, (c + 1) * STRETCH)
            tails = jnp.concatenate([by_lane(tail_cols[c], pair) for pair in (2 * g, 2 * g + 1)], axis=1)
            weighted = (inner[at, columns].astype(F32) * tails).astype(BF16)
            contrib[c, :, columns] = dot(write_turned[c], weighted)

        @pl.when(me < tm_count - 1)
        def _(g=g):
            for pair in (2 * g, 2 * g + 1):
                take_state(pair)
                s_copy(pair).start()

    grams = [dot(read_vecs[c], write_vecs[c], ((1,), (1,))) for c in range(blocks)]

    def within_of(pair):
        within = []
        for c in range(blocks):
            at = slice(c * STRETCH, (c + 1) * STRETCH)
            entries = inner[at, tile(pair)]
            parts = []
            for h in (2 * pair, 2 * pair + 1):
                matrix = decays[c, h] * grams[c]
                parts.append(dot(matrix.astype(BF16), entries))
            within.append(jnp.where(low_lane, parts[0], parts[1]))
        return within

    ready = [within_of(pair) for pair in range(state_pairs)]
    for pair in range(state_pairs):

        @pl.when(me == tm_count - 1)
        def _(pair=pair):
            take_state(pair)

        for c in range(blocks):
            at = slice(c * STRETCH, (c + 1) * STRETCH)
            carried = dot(read_vecs[c], states[c, :, tile(pair)]) * by_lane(grow_cols[c], pair)
            out_ref[0, at, tile(pair)] = (ready[pair][c] + carried).astype(BF16)

    @pl.when(me < tm_count - 1)
    def _():
        halo_copy.wait_send()
        for pair in range(state_pairs):
            s_copy(pair).wait_send()

    if hub:
        for p in range(pairs):

            @pl.when(me >= 2)
            def _(p=p):
                q_copy(p, asker).wait_send()

            @pl.when(me == 3)
            def _(p=p):
                q_copy(p, 0, 2).wait_send()

            @pl.when(me == 0)
            def _(p=p):
                kv_copy(p).wait_send()

            @pl.when((me == 1) | (me == 2))
            def _(p=p):
                part_copy(p, 0, 3, 0).wait_send()

            @pl.when(me == 1)
            def _(p=p):
                part_copy(p, 1, 3, 0).wait_send()


def solution(mesh):
    grp_count, tm_count, seq_count, sub_count = (
        mesh.shape[axis] for axis in ("grp", "tm", "seq", "sub")
    )

    def on_device(
        queries,
        key_proj,
        value_proj,
        residual,
        mix_weight,
        inner_weight,
        write_weight,
        read_weight,
        step_logits,
        decay_rates,
        carried_state,
        carried_valid,
    ):
        rows, columns = queries.shape[1:]
        width = residual.shape[2]
        heads, channels, state_dim = carried_state.shape[1:]
        assert rows == 2 * STRIDE and state_dim == LANES and channels == HALF
        pairs = columns // LANES
        share = STRIDE // tm_count
        inner_columns = inner_weight.shape[1]
        state_pairs = heads // 2
        carried = carried_state.reshape(1, heads * channels, state_dim)
        vmem = pl.BlockSpec(memory_space=pltpu.VMEM)
        smem = pl.BlockSpec(memory_space=pltpu.SMEM)
        anywhere = pl.BlockSpec(memory_space=pl.ANY)
        dma = pltpu.SemaphoreType.DMA
        pieces = 3 + inner_columns // (2 * LANES)
        if tm_count == 4:
            strided = (
                pltpu.VMEM((pairs, STRIDE, LANES), BF16),
                pltpu.VMEM((pairs, 2, STRIDE, LANES), BF16),
                pltpu.VMEM((2, pairs, STRIDE, LANES), BF16),
                pltpu.VMEM((pairs, 2, STRIDE, LANES), BF16),
                pltpu.VMEM((2, pairs, STRIDE + 32, LANES), BF16),
                pltpu.VMEM((2, pairs, STRIDE + 32, LANES), BF16),
                pltpu.VMEM((3, pairs, STRIDE, LANES), F32),
            )
            strided_sems = tuple(
                dma(extent)
                for extent in ((2 * pairs,), (2, pairs), (pairs,), (pairs,), (2, pairs), (2, pairs))
            )
        else:
            strided = (
                pltpu.VMEM((STRIDE, 3 * columns), BF16),
                pltpu.VMEM((tm_count, share, 3 * columns), BF16),
                pltpu.VMEM((tm_count, share, columns), BF16),
            )
            strided_sems = tuple(
                dma(extent)
                for extent in ((tm_count,), (tm_count,), (pairs, tm_count), (pairs, tm_count))
            )
        return pl.pallas_call(
            functools.partial(layer, grp_count, tm_count, seq_count, sub_count),
            out_shape=(
                pltpu.VMEM((1, rows, width), BF16),
                pltpu.VMEM((1, rows, inner_columns), BF16),
            ),
            in_specs=[anywhere] * 10 + [smem] * 2,
            out_specs=(vmem, vmem),
            scratch_shapes=[
                pltpu.VMEM((1, rows, columns), BF16),
                pltpu.VMEM((1, rows, columns), BF16),
                pltpu.VMEM((1, rows, columns), BF16),
                pltpu.VMEM((1, rows, width), BF16),
                pltpu.VMEM((heads, 1, rows), F32),
                pltpu.VMEM((1, heads * channels, state_dim), F32),
                strided,
                strided_sems,
                pltpu.VMEM((STRIDE, columns), BF16),
                pltpu.VMEM((STRIDE, columns), BF16),
                pltpu.VMEM((STRIDE, columns), BF16),
                pltpu.VMEM((rows, columns), BF16),
                pltpu.VMEM((seq_count,) + mix_weight.shape, BF16),
                pltpu.VMEM((inner_columns // (2 * LANES), width, 2 * LANES), BF16),
                pltpu.VMEM((width, state_dim), BF16),
                pltpu.VMEM((width, state_dim), BF16),
                pltpu.VMEM((rows, width), BF16),
                pltpu.VMEM((max(sub_count - 1, 1), rows, width), BF16),
                pltpu.VMEM((rows, width), BF16),
                pltpu.VMEM((rows, inner_columns), BF16),
                pltpu.VMEM((rows // STRETCH, state_dim, heads * channels), F32),
                pltpu.VMEM((rows // STRETCH, heads, STRETCH, STRETCH), F32),
                pltpu.VMEM((rows // STRETCH, state_dim, heads * channels), BF16),
                pltpu.VMEM((state_dim, heads * channels), F32),
                pltpu.VMEM((state_pairs, LANES, state_dim), BF16),
                pltpu.VMEM((state_pairs, LANES, state_dim), BF16),
                dma((1,)),
                dma((1,)),
                dma((pieces, seq_count)),
                dma((pieces, seq_count)),
                dma((pieces, seq_count, grp_count)),
                dma((pieces, seq_count, grp_count)),
                dma((rows // STRIDE, sub_count)),
                dma((rows // STRIDE, sub_count)),
                dma((state_pairs,)),
                dma((state_pairs,)),
                dma((pieces + 6,)),
            ],
            compiler_params=pltpu.CompilerParams(
                collective_id=0, has_side_effects=True, vmem_limit_bytes=60 * 1024 * 1024
            ),
        )(
            queries,
            key_proj,
            value_proj,
            residual,
            mix_weight,
            inner_weight,
            write_weight,
            read_weight,
            jnp.transpose(step_logits, (1, 0, 2)),
            carried,
            decay_rates,
            carried_valid,
        )

    in_specs = (
        P(("grp", "seq"), "tm", "sub"),
        P(("grp", "seq"), "tm", "sub"),
        P(("grp", "seq"), "tm", "sub"),
        P(("grp", "seq"), "tm", None),
        P("sub", "seq"),
        P("seq", "sub"),
        P("seq", None),
        P("seq", None),
        P(("grp", "seq"), "sub", "tm"),
        P("sub"),
        P(("grp", "seq"), "sub", None, None),
        P(("grp", "seq"), "sub"),
    )
    out_specs = (P(("grp", "seq"), "tm", None), P(("grp", "seq"), "tm", "sub"))
    return jax.shard_map(
        on_device, mesh=mesh, in_specs=in_specs, out_specs=out_specs, check_vma=False
    )
```

```python
import functools

import jax
import jax.numpy as jnp
from jax import lax
from jax.experimental import pallas as pl
from jax.experimental.pallas import tpu as pltpu
from jax.sharding import PartitionSpec as P

MESH = pl.DeviceIdType.MESH
LANES = 128
HALF = 64
STRIDE = 256
STRETCH = 128
SCALE = 0.125
NEGATIVE = -1e30
EPSILON = 1e-05
F32 = jnp.float32
BF16 = jnp.bfloat16


def dot(a, b, contract=((1,), (0,)), precision=None):
    return lax.dot_general(
        a, b, (contract, ((), ())), precision=precision, preferred_element_type=F32
    )


def tile(index):
    return slice(index * LANES, (index + 1) * LANES)


def softplus(x):
    e = jnp.exp(-jnp.abs(x))
    u = 1.0 + e
    low = jnp.where(u == 1.0, e, jnp.log(u) * e / jnp.where(u == 1.0, 1.0, u - 1.0))
    return jnp.maximum(x, 0.0) + low


def layer(
    grp_count,
    tm_count,
    seq_count,
    sub_count,
    q_hbm,
    k_hbm,
    v_hbm,
    res_hbm,
    mix_ref,
    inw_ref,
    ww_ref,
    rw_ref,
    logit_hbm,
    carry_hbm,
    rates_ref,
    valid_ref,
    stream_ref,
    out_ref,
    q_ref,
    k_ref,
    v_ref,
    res_ref,
    logit_ref,
    carry_ref,
    strided,
    strided_sems,
    o_in,
    halo_out,
    halo_in,
    mixed,
    mix_all,
    inw_all,
    ww_all,
    rw_all,
    b_out,
    b_in,
    normed,
    inner,
    contrib,
    decays,
    states,
    first,
    s_out,
    s_in,
    h_send,
    h_recv,
    w_send,
    w_recv,
    f_send,
    f_recv,
    b_send,
    b_recv,
    s_send,
    s_recv,
    l_sem,
):
    me = lax.axis_index("tm")
    my_seq = lax.axis_index("seq")
    my_sub = lax.axis_index("sub")
    my_grp = lax.axis_index("grp")
    pairs = q_ref.shape[2] // LANES
    rows = q_ref.shape[1]
    width = res_ref.shape[2]
    share = STRIDE // tm_count
    heads = rates_ref.shape[0]
    state_pairs = heads // 2
    blocks = rows // STRETCH

    in_rows = inw_ref.shape[0]
    mine = pl.ds(pl.multiple_of(my_seq * in_rows, in_rows), in_rows)

    def peers(axis, mine, count):
        return [(d, {axis: lax.rem(mine + d, count)}) for d in range(1, count)]

    tm_peers = peers("tm", me, tm_count)
    seq_peers = peers("seq", my_seq, seq_count)
    sub_peers = peers("sub", my_sub, sub_count)
    grp_peers = peers("grp", my_grp, grp_count)
    barrier = pltpu.get_barrier_semaphore()
    hub = tm_count == 4
    greeted = seq_peers + sub_peers + grp_peers + ([] if hub else tm_peers)
    for _, peer in greeted:
        pl.semaphore_signal(barrier, inc=1, device_id=peer, device_id_type=MESH)
    arrivals = len(greeted)
    if hub:
        arrivals = arrivals + jnp.where(me == 0, 1, jnp.where(me == 1, 3, 2))
        for t in range(tm_count):
            apart = (me == t) | ((me == 0) & (t >= 2)) | ((me >= 2) & (t == 0))

            @pl.when(~apart)
            def _(t=t):
                pl.semaphore_signal(barrier, inc=1, device_id={"tm": t}, device_id_type=MESH)

    group = 2 * LANES
    groups = inw_ref.shape[1] // group
    moves = [("q", q_hbm, q_ref), ("k", k_hbm, k_ref), ("v", v_hbm, v_ref)]
    moves += [("mix", mix_ref, mix_all.at[my_seq])]
    moves += [("ww", ww_ref, ww_all.at[mine]), ("rw", rw_ref, rw_all.at[mine])]
    moves += [
        ("inw%d" % g, inw_ref.at[:, g * group : (g + 1) * group], inw_all.at[g, mine])
        for g in range(groups)
    ]
    moves += [("logit", logit_hbm, logit_ref), ("res", res_hbm, res_ref)]
    moves += [("carry", carry_hbm, carry_ref)]
    loads = {
        name: pltpu.make_async_copy(src, dst, l_sem.at[index])
        for index, (name, src, dst) in enumerate(moves)
    }
    for load in loads.values():
        load.start()
    loads["q"].wait()
    if not hub:
        loads["k"].wait()
        loads["v"].wait()
    low_half = lax.broadcasted_iota(jnp.int32, (STRIDE, LANES), 1) < HALF

    if hub:
        q_out, kv_out, q_in, kv_in, part_out, part_in, own_part = strided
        q_send, q_recv, kv_send, kv_recv, p_send, p_recv = strided_sems
    else:
        x_out, x_in, o_out = strided
        x_send, x_recv, o_send, o_recv = strided_sems

    def packed(ref, p):
        first_half = pltpu.roll(ref[0, :STRIDE, tile(p)].astype(F32), HALF, 1)
        second_half = ref[0, STRIDE:, tile(p)].astype(F32)
        return jnp.where(low_half, first_half, second_half).astype(BF16)

    for p in range(pairs):
        if hub:
            q_out[p] = packed(q_ref, p)
        else:
            for which, ref in enumerate((q_ref, k_ref, v_ref)):
                x_out[:, tile(which * pairs + p)] = packed(ref, p)

    def remote(src, dst, send, recv, peer):
        return pltpu.make_async_remote_copy(
            src_ref=src,
            dst_ref=dst,
            send_sem=send,
            recv_sem=recv,
            device_id=peer,
            device_id_type=MESH,
        )

    pl.semaphore_wait(barrier, arrivals)
    ahead = jnp.minimum(me + 1, tm_count - 1)
    if hub:
        asker = jnp.maximum(me - 2, 0)

        def q_copy(p, slot, to=1):
            sent = q_send.at[p] if to == 1 else q_send.at[pairs + p]
            return remote(q_out.at[p], q_in.at[slot, p], sent, q_recv.at[slot, p], {"tm": to})

        def kv_copy(p):
            return remote(kv_out.at[p], kv_in.at[p], kv_send.at[p], kv_recv.at[p], {"tm": 1})

        def part_copy(p, slot, to, place):
            return remote(
                part_out.at[slot, p],
                part_in.at[place, p],
                p_send.at[slot, p],
                p_recv.at[place, p],
                {"tm": to},
            )

        for p in range(pairs):

            @pl.when(me >= 2)
            def _(p=p):
                q_copy(p, asker).start()

        loads["k"].wait()
        loads["v"].wait()
        for p in range(pairs):
            kv_out[p, 0] = packed(k_ref, p)
            kv_out[p, 1] = packed(v_ref, p)

            @pl.when((me == 0) & (p < pairs - 1))
            def _(p=p):
                kv_copy(p).start()

    for p in range(pairs):
        key_tail = k_ref[0, rows - STRIDE :, tile(p)].astype(F32)
        value_tail = pltpu.roll(v_ref[0, rows - STRIDE :, tile(p)].astype(F32), HALF, 1)
        halo_out[:, tile(p)] = jnp.where(low_half, key_tail, value_tail).astype(BF16)

    @pl.when(me == 0)
    def _():
        halo_in[...] = jnp.zeros_like(halo_in)

    def residues(index):
        return pl.ds(pl.multiple_of(index * share, share), share)

    halo_copy = remote(halo_out, halo_in, h_send.at[0], h_recv.at[0], {"tm": ahead})
    if not hub:
        x_copies = [
            remote(
                x_out.at[residues(peer["tm"])], x_in.at[me], x_send.at[d], x_recv.at[d], peer
            )
            for d, peer in tm_peers
        ]
        for copy in x_copies:
            copy.start()

    @pl.when(me < tm_count - 1)
    def _():
        halo_copy.start()

    if hub:

        @pl.when(me == 0)
        def _():
            kv_copy(pairs - 1).start()

        for p in range(pairs):

            @pl.when(me == 3)
            def _(p=p):
                q_copy(p, 0, 2).start()

    pieces = ["mix", "ww", "rw"] + ["inw%d" % g for g in range(groups)]

    def region(index, owner):
        if index == 0:
            part = mix_ref.shape[0] // grp_count
            return mix_all.at[owner, pl.ds(pl.multiple_of(my_grp * part, part), part)]
        part = in_rows // grp_count
        at = pl.ds(pl.multiple_of(owner * in_rows + my_grp * part, part), part)
        return (ww_all, rw_all)[index - 1].at[at] if index < 3 else inw_all.at[index - 3, at]

    w_copies, f_copies = [], []
    for index, name in enumerate(pieces):
        loads[name].wait()
        own = region(index, my_seq)
        w_copies.append(
            [
                remote(own, own, w_send.at[index, d], w_recv.at[index, d], peer)
                for d, peer in seq_peers
            ]
        )
        f_copies.append([])
        for d, _ in seq_peers:
            place = region(index, lax.rem(my_seq - d + seq_count, seq_count))
            for e, peer in grp_peers:
                f_copies[-1].append(
                    remote(place, place, f_send.at[index, d, e], f_recv.at[index, d, e], peer)
                )
        for copy in w_copies[-1]:
            copy.start()

    def pass_on(index):
        for copy in w_copies[index]:
            copy.wait()
        for copy in f_copies[index]:
            copy.start()

    if not hub:
        x_in[me] = x_out[residues(me), :]

    row_at = lax.broadcasted_iota(jnp.int32, (STRIDE, STRIDE), 0)
    col_at = lax.broadcasted_iota(jnp.int32, (STRIDE, STRIDE), 1)
    own_allowed = col_at <= row_at

    def near(block, prev_keys, prev_values, prev_allowed, turned):
        at = slice(block * STRIDE, (block + 1) * STRIDE)
        for p in range(pairs):
            query = jnp.where(low_half, q_ref[0, at, tile(p)].astype(F32) * SCALE, 0.0).astype(BF16)
            own = dot(query, k_ref[0, at, tile(p)], ((1,), (1,)))
            prev = dot(query, prev_keys(p), ((1,), (1,)))
            own = jnp.where(own_allowed, own, NEGATIVE)
            prev = jnp.where(prev_allowed, prev, NEGATIVE)
            top = jnp.maximum(
                jnp.max(own, axis=1, keepdims=True), jnp.max(prev, axis=1, keepdims=True)
            )
            own = jnp.where(own_allowed, jnp.exp(own - top), 0.0)
            prev = jnp.where(prev_allowed, jnp.exp(prev - top), 0.0)
            total = jnp.sum(own, axis=1, keepdims=True) + jnp.sum(prev, axis=1, keepdims=True)
            from_prev = dot(prev.astype(BF16), prev_values(p))
            if turned:
                from_prev = pltpu.roll(from_prev, HALF, 1)
            result = dot(own.astype(BF16), v_ref[0, at, tile(p)]) + from_prev
            mixed[at, tile(p)] = (result / total).astype(BF16)

    def first_block():
        @pl.when(me > 0)
        def _():
            halo_copy.wait_recv()

        near(
            0,
            lambda p: halo_in[:, tile(p)],
            lambda p: halo_in[:, tile(p)],
            (col_at > row_at) & (me > 0),
            True,
        )

    near(
        1,
        lambda p: k_ref[0, :STRIDE, tile(p)],
        lambda p: v_ref[0, :STRIDE, tile(p)],
        col_at > row_at,
        False,
    )

    loads["logit"].wait()
    head_at = lax.broadcasted_iota(jnp.int32, (heads, 1), 0)
    rates = jnp.zeros((heads, 1), F32)
    flags = jnp.zeros((heads, 1), F32)
    for h in range(heads):
        rates = jnp.where(head_at == h, rates_ref[h], rates)
        flags = jnp.where(head_at == h, valid_ref[0, h].astype(F32), flags)
    step = softplus(logit_ref[:, 0, :])
    log_decay = -rates * step
    tri = (
        lax.broadcasted_iota(jnp.int32, (STRETCH, STRETCH), 0)
        <= lax.broadcasted_iota(jnp.int32, (STRETCH, STRETCH), 1)
    ).astype(F32)
    step_rows, cum_rows, cum_cols, grow_cols, tail_cols, block_decay = [], [], [], [], [], []
    for c in range(blocks):
        at = slice(c * STRETCH, (c + 1) * STRETCH)
        cum = dot(log_decay[:, at], tri, precision=lax.Precision.HIGHEST)
        last = cum[:, STRETCH - 1 :]
        tail = jnp.exp(last - cum) * step[:, at]
        step_rows.append(step[:, at])
        cum_rows.append(cum)
        cum_cols.append(jnp.transpose(cum))
        grow_cols.append(jnp.exp(cum_cols[-1]))
        tail_cols.append(jnp.transpose(tail))
        block_decay.append(jnp.exp(last))

    low_lane = lax.broadcasted_iota(jnp.int32, (STRETCH, LANES), 1) < HALF
    low_row = low_lane[:1]

    def over_lanes(entries, pair):
        return jnp.where(low_row, entries[2 * pair : 2 * pair + 1], entries[2 * pair + 1 : 2 * pair + 2])

    loads["carry"].wait()
    for pair in range(state_pairs):
        valid = over_lanes(flags, pair) != 0.0
        first[:, tile(pair)] = jnp.where(valid, jnp.transpose(carry_ref[0, tile(pair), :]), 0.0)

    causal = lax.broadcasted_iota(jnp.int32, (STRETCH, STRETCH), 0) >= lax.broadcasted_iota(
        jnp.int32, (STRETCH, STRETCH), 1
    )
    for c in range(blocks):
        for h in range(heads):
            distance = cum_cols[c][:, h : h + 1] - cum_rows[c][h : h + 1, :]
            decay = jnp.exp(jnp.where(causal, distance, NEGATIVE))
            decays[c, h] = decay * step_rows[c][h : h + 1, :]

    pass_on(0)
    if not hub:
        for index in range(1, len(pieces)):
            pass_on(index)
        for copy in x_copies:
            copy.wait()
    ones = (
        (lax.broadcasted_iota(jnp.int32, (LANES, LANES), 0) < HALF)
        == (lax.broadcasted_iota(jnp.int32, (LANES, LANES), 1) < HALF)
    ).astype(BF16)
    if hub:
        upper = ~low_half
        stat_row = lax.broadcasted_iota(jnp.int32, (16, 3 * LANES), 0)
        stat_lane = lax.broadcasted_iota(jnp.int32, (16, 3 * LANES), 1)
        stat_pick = (
            (stat_row < 6) & (stat_lane == (stat_row // 2) * LANES + (stat_row % 2) * HALF)
        ).astype(BF16)
        back_row = lax.broadcasted_iota(jnp.int32, (16, LANES), 0)
        back_low = lax.broadcasted_iota(jnp.int32, (16, LANES), 1) < HALF
        stat_back = ((back_row < 6) & ((back_row % 2 == 0) == back_low)).astype(BF16)

        def lane_sums(product):
            high = product.astype(BF16)
            low = (product - high.astype(F32)).astype(BF16)
            return dot(high, ones) + dot(low, ones)

        def with_turned(ref, p):
            keys, values = ref[p, 0].astype(F32), ref[p, 1].astype(F32)
            return keys, pltpu.roll(keys, HALF, 1), values, pltpu.roll(values, HALF, 1)

        def attend(query, sets, diagonal):
            scores = []
            for index, (keys, keys_turned, _, _) in enumerate(sets):
                straight, turned = lane_sums(keys * query), lane_sums(keys_turned * query)
                if diagonal and index == 0:
                    turned = jnp.where(upper, turned, NEGATIVE)
                scores.append((straight, turned))
            top = functools.reduce(jnp.maximum, [jnp.maximum(*pair) for pair in scores])
            total, result = 0.0, 0.0
            for index, (_, _, values, values_turned) in enumerate(sets):
                straight, turned = (jnp.exp(entry - top) for entry in scores[index])
                if diagonal and index == 0:
                    turned = jnp.where(upper, turned, 0.0)
                total = total + (straight + turned)
                result = result + (
                    straight.astype(BF16).astype(F32) * values
                    + turned.astype(BF16).astype(F32) * values_turned
                )
            return result, total, top

        def keep(p, sets):
            outcome = attend(q_out[p].astype(F32) * SCALE, sets, True)
            for index, entry in enumerate(outcome):
                own_part[index, p] = entry

        def serve(p, slot, sets, to, place):
            q_copy(p, slot).wait_recv()
            result, total, top = attend(q_in[slot, p].astype(F32) * SCALE, sets, False)
            part_out[slot, p, :STRIDE] = (result / total).astype(BF16)
            log_sum = top + jnp.log(total)
            high = log_sum.astype(BF16)
            left = log_sum - high.astype(F32)
            middle = left.astype(BF16)
            low = (left - middle.astype(F32)).astype(BF16)
            stats = dot(
                stat_pick, jnp.concatenate([high, middle, low], axis=1), ((1,), (1,))
            ).astype(BF16)
            part_out[slot, p, STRIDE : STRIDE + 16] = stats[:, :LANES]
            part_out[slot, p, STRIDE + 16 :] = stats[:, LANES:]
            part_copy(p, slot, to, place).start()

        pass_at = {0: (1, 2)}
        for p in range(pairs):
            if p == pairs - 1:
                first_block()
                pass_on(3)

            @pl.when(me == 1)
            def _(p=p):
                kv_copy(p).wait_recv()
                sets = (with_turned(kv_out, p), with_turned(kv_in, p))
                for slot in range(2):
                    serve(p, slot, sets, 2 + slot, 0)
                keep(p, sets)

            @pl.when(me == 2)
            def _(p=p):
                sets = (with_turned(kv_out, p),)
                serve(p, 0, sets, 3, 1)
                keep(p, sets)

            @pl.when((me == 0) | (me == 3))
            def _(p=p):
                keep(p, (with_turned(kv_out, p),))

            for index in pass_at.get(p, ()):
                pass_on(index)
    else:
        source = lax.broadcasted_iota(jnp.int32, (tm_count, share, LANES), 0)
        upper = lax.broadcasted_iota(jnp.int32, (tm_count, share, LANES), 2) >= HALF
        full = (tm_count * share, LANES)
        cube = (tm_count, share, LANES)

        def lane_sums(product):
            product = product.reshape(full)
            high = product.astype(BF16)
            low = (product - high.astype(F32)).astype(BF16)
            return (dot(high, ones) + dot(low, ones)).reshape(cube)

        o_copies = []
        for p in range(pairs):
            keys = x_in[:, :, tile(pairs + p)].astype(F32)
            values = x_in[:, :, tile(2 * pairs + p)].astype(F32)
            keys_turned = pltpu.roll(keys.reshape(full), HALF, 1).reshape(cube)
            values_turned = pltpu.roll(values.reshape(full), HALF, 1).reshape(cube)

            def far(d, carry, p=p, keys=keys, values=values, kt=keys_turned, vt=values_turned):
                query = x_in[d, :, tile(p)].astype(F32)[None] * SCALE
                allowed = source <= d
                allowed_turned = (source < d) | ((source == d) & upper)
                straight = jnp.where(allowed, lane_sums(keys * query), NEGATIVE)
                turned = jnp.where(allowed_turned, lane_sums(kt * query), NEGATIVE)
                top = jnp.max(jnp.maximum(straight, turned), axis=0, keepdims=True)
                straight = jnp.where(allowed, jnp.exp(straight - top), 0.0)
                turned = jnp.where(allowed_turned, jnp.exp(turned - top), 0.0)
                total = jnp.sum(straight + turned, axis=0)
                result = jnp.sum(
                    straight.astype(BF16).astype(F32) * values + turned.astype(BF16).astype(F32) * vt,
                    axis=0,
                )
                o_out[d, :, tile(p)] = (result / total).astype(BF16)
                return carry

            lax.fori_loop(0, tm_count, far, 0, unroll=tm_count <= 4)

            for d, peer in tm_peers:
                o_copies.append(
                    remote(
                        o_out.at[peer["tm"], :, tile(p)],
                        o_in.at[residues(me), tile(p)],
                        o_send.at[p, d],
                        o_recv.at[p, d],
                        peer,
                    )
                )
                o_copies[-1].start()

        o_in[residues(me), :] = o_out[me]

    if not hub:
        first_block()
    if hub:
        for index in range(4, len(pieces) - 1):
            pass_on(index)
        for p in range(pairs):
            if p == pairs - 1:

                @pl.when(me >= 2)
                def _():
                    pass_on(len(pieces) - 1)


            @pl.when(me < 2)
            def _(p=p):
                o_in[:, tile(p)] = (own_part[0, p] / own_part[1, p]).astype(BF16)

            for count, condition in ((1, me == 2), (2, me == 3)):

                @pl.when(condition)
                def _(p=p, count=count):
                    log_sums = []
                    for place in range(count):
                        part_copy(p, 0, 2, place).wait_recv()
                        halves = [
                            part_in[place, p, STRIDE + 16 * half : STRIDE + 16 * (half + 1)]
                            for half in range(2)
                        ]
                        log_sums.append(
                            jnp.concatenate(
                                [dot(half, stat_back, ((0,), (0,))) for half in halves], axis=0
                            )
                        )
                    top = functools.reduce(jnp.maximum, log_sums, own_part[2, p])
                    scale = jnp.exp(own_part[2, p] - top)
                    result, total = own_part[0, p] * scale, own_part[1, p] * scale
                    for place in range(count):
                        scale = jnp.exp(log_sums[place] - top)
                        result = result + part_in[place, p, :STRIDE].astype(F32) * scale
                        total = total + scale
                    o_in[:, tile(p)] = (result / total).astype(BF16)
    else:
        for copy in o_copies:
            copy.wait()
    for copy in f_copies[0]:
        copy.wait()

    piece = mix_ref.shape[1]
    b_copies = []
    for a in range(rows // STRIDE):
        at = slice(a * STRIDE, (a + 1) * STRIDE)
        for p in range(pairs):
            far_part = o_in[:, tile(p)].astype(F32)
            if a == 0:
                far_part = pltpu.roll(far_part, HALF, 1)
            mixed[at, tile(p)] = jnp.where(
                low_half, mixed[at, tile(p)].astype(F32), far_part
            ).astype(BF16)
        if piece % LANES == 0:
            for s in range(seq_count):
                b_out[at, s * piece : (s + 1) * piece] = dot(mixed[at, :], mix_all[s]).astype(BF16)
        else:
            total = jnp.zeros((STRIDE, width), F32)
            from_col = lax.broadcasted_iota(jnp.int32, (piece, width), 0)
            to_col = lax.broadcasted_iota(jnp.int32, (piece, width), 1)
            for s in range(seq_count):
                placed = (to_col == from_col + s * piece).astype(BF16)
                weight = dot(mix_all[s], placed).astype(BF16)
                total = total + dot(mixed[at, :], weight)
            b_out[at, :] = total.astype(BF16)
        b_copies.append(
            [
                remote(
                    b_out.at[pl.ds(a * STRIDE, STRIDE)],
                    b_in.at[d - 1, pl.ds(a * STRIDE, STRIDE)],
                    b_send.at[a, d],
                    b_recv.at[a, d],
                    peer,
                )
                for d, peer in sub_peers
            ]
        )
        for copy in b_copies[-1]:
            copy.start()
    if hub:

        @pl.when(me < 2)
        def _():
            pass_on(len(pieces) - 1)

    loads["res"].wait()
    for index in (1, 2):
        for copy in f_copies[index]:
            copy.wait()
    read_vecs, write_vecs, write_turned = [], [], []
    for a in range(rows // STRIDE):
        at = slice(a * STRIDE, (a + 1) * STRIDE)
        for copy in b_copies[a]:
            copy.wait()
        branch = b_out[at, :].astype(F32)
        for d, _ in sub_peers:
            branch = branch + b_in[d - 1, at, :].astype(F32)
        stream = (res_ref[0, at, :].astype(F32) + branch).astype(BF16)
        stream_ref[0, at, :] = stream
        wide = stream.astype(F32)
        mean = jnp.sum(wide * wide, axis=1, keepdims=True) * (1.0 / width)
        normed[at, :] = (wide * lax.rsqrt(mean + EPSILON)).astype(BF16)
        write_vec = dot(normed[at, :], ww_all[...]).astype(BF16)
        read_vec = dot(normed[at, :], rw_all[...]).astype(BF16)
        for c in range(STRIDE // STRETCH):
            write_vecs.append(write_vec[c * STRETCH : (c + 1) * STRETCH])
            write_turned.append(jnp.transpose(write_vecs[-1].astype(F32)).astype(BF16))
            read_vecs.append(read_vec[c * STRETCH : (c + 1) * STRETCH])
    def by_lane(cols, pair):
        return jnp.where(
            low_lane, cols[:, 2 * pair : 2 * pair + 1], cols[:, 2 * pair + 1 : 2 * pair + 2]
        )

    def s_copy(pair):
        return remote(
            s_out.at[pair], s_in.at[pair], s_send.at[pair], s_recv.at[pair], {"tm": ahead}
        )

    def take_state(pair):
        @pl.when(me > 0)
        def _():
            s_copy(pair).wait_recv()

        @pl.when(me == 0)
        def _():
            s_in[pair] = first[:, tile(pair)].astype(BF16)

        state = jnp.where(me == 0, first[:, tile(pair)], s_in[pair].astype(F32))
        for c in range(blocks):
            states[c, :, tile(pair)] = state.astype(BF16)
            state = over_lanes(block_decay[c], pair) * state + contrib[c, :, tile(pair)]
        s_out[pair] = state.astype(BF16)

    for g in range(groups):
        columns = slice(g * group, (g + 1) * group)
        for copy in f_copies[3 + g]:
            copy.wait()
        for a in range(rows // STRIDE):
            at = slice(a * STRIDE, (a + 1) * STRIDE)
            drive = dot(normed[at, :], inw_all[g])
            inner[at, columns] = (drive / (1.0 + jnp.exp(-drive))).astype(BF16)
        for c in range(blocks):
            at = slice(c * STRETCH, (c + 1) * STRETCH)
            tails = jnp.concatenate([by_lane(tail_cols[c], pair) for pair in (2 * g, 2 * g + 1)], axis=1)
            weighted = (inner[at, columns].astype(F32) * tails).astype(BF16)
            contrib[c, :, columns] = dot(write_turned[c], weighted)

        @pl.when(me < tm_count - 1)
        def _(g=g):
            for pair in (2 * g, 2 * g + 1):
                take_state(pair)
                s_copy(pair).start()

    grams = [dot(read_vecs[c], write_vecs[c], ((1,), (1,))) for c in range(blocks)]

    def within_of(pair):
        within = []
        for c in range(blocks):
            at = slice(c * STRETCH, (c + 1) * STRETCH)
            entries = inner[at, tile(pair)]
            parts = []
            for h in (2 * pair, 2 * pair + 1):
                matrix = decays[c, h] * grams[c]
                parts.append(dot(matrix.astype(BF16), entries))
            within.append(jnp.where(low_lane, parts[0], parts[1]))
        return within

    ready = [within_of(pair) for pair in range(state_pairs)]
    for pair in range(state_pairs):

        @pl.when(me == tm_count - 1)
        def _(pair=pair):
            take_state(pair)

        for c in range(blocks):
            at = slice(c * STRETCH, (c + 1) * STRETCH)
            carried = dot(read_vecs[c], states[c, :, tile(pair)]) * by_lane(grow_cols[c], pair)
            out_ref[0, at, tile(pair)] = (ready[pair][c] + carried).astype(BF16)

    @pl.when(me < tm_count - 1)
    def _():
        halo_copy.wait_send()
        for pair in range(state_pairs):
            s_copy(pair).wait_send()

    if hub:
        for p in range(pairs):

            @pl.when(me >= 2)
            def _(p=p):
                q_copy(p, asker).wait_send()

            @pl.when(me == 3)
            def _(p=p):
                q_copy(p, 0, 2).wait_send()

            @pl.when(me == 0)
            def _(p=p):
                kv_copy(p).wait_send()

            @pl.when((me == 1) | (me == 2))
            def _(p=p):
                part_copy(p, 0, 3, 0).wait_send()

            @pl.when(me == 1)
            def _(p=p):
                part_copy(p, 1, 3, 0).wait_send()


def solution(mesh):
    grp_count, tm_count, seq_count, sub_count = (
        mesh.shape[axis] for axis in ("grp", "tm", "seq", "sub")
    )

    def on_device(
        queries,
        key_proj,
        value_proj,
        residual,
        mix_weight,
        inner_weight,
        write_weight,
        read_weight,
        step_logits,
        decay_rates,
        carried_state,
        carried_valid,
    ):
        rows, columns = queries.shape[1:]
        width = residual.shape[2]
        heads, channels, state_dim = carried_state.shape[1:]
        assert rows == 2 * STRIDE and state_dim == LANES and channels == HALF
        pairs = columns // LANES
        share = STRIDE // tm_count
        inner_columns = inner_weight.shape[1]
        state_pairs = heads // 2
        carried = carried_state.reshape(1, heads * channels, state_dim)
        vmem = pl.BlockSpec(memory_space=pltpu.VMEM)
        smem = pl.BlockSpec(memory_space=pltpu.SMEM)
        anywhere = pl.BlockSpec(memory_space=pl.ANY)
        dma = pltpu.SemaphoreType.DMA
        pieces = 3 + inner_columns // (2 * LANES)
        if tm_count == 4:
            strided = (
                pltpu.VMEM((pairs, STRIDE, LANES), BF16),
                pltpu.VMEM((pairs, 2, STRIDE, LANES), BF16),
                pltpu.VMEM((2, pairs, STRIDE, LANES), BF16),
                pltpu.VMEM((pairs, 2, STRIDE, LANES), BF16),
                pltpu.VMEM((2, pairs, STRIDE + 32, LANES), BF16),
                pltpu.VMEM((2, pairs, STRIDE + 32, LANES), BF16),
                pltpu.VMEM((3, pairs, STRIDE, LANES), F32),
            )
            strided_sems = tuple(
                dma(extent)
                for extent in ((2 * pairs,), (2, pairs), (pairs,), (pairs,), (2, pairs), (2, pairs))
            )
        else:
            strided = (
                pltpu.VMEM((STRIDE, 3 * columns), BF16),
                pltpu.VMEM((tm_count, share, 3 * columns), BF16),
                pltpu.VMEM((tm_count, share, columns), BF16),
            )
            strided_sems = tuple(
                dma(extent)
                for extent in ((tm_count,), (tm_count,), (pairs, tm_count), (pairs, tm_count))
            )
        return pl.pallas_call(
            functools.partial(layer, grp_count, tm_count, seq_count, sub_count),
            out_shape=(
                pltpu.VMEM((1, rows, width), BF16),
                pltpu.VMEM((1, rows, inner_columns), BF16),
            ),
            in_specs=[anywhere] * 10 + [smem] * 2,
            out_specs=(vmem, vmem),
            scratch_shapes=[
                pltpu.VMEM((1, rows, columns), BF16),
                pltpu.VMEM((1, rows, columns), BF16),
                pltpu.VMEM((1, rows, columns), BF16),
                pltpu.VMEM((1, rows, width), BF16),
                pltpu.VMEM((heads, 1, rows), F32),
                pltpu.VMEM((1, heads * channels, state_dim), F32),
                strided,
                strided_sems,
                pltpu.VMEM((STRIDE, columns), BF16),
                pltpu.VMEM((STRIDE, columns), BF16),
                pltpu.VMEM((STRIDE, columns), BF16),
                pltpu.VMEM((rows, columns), BF16),
                pltpu.VMEM((seq_count,) + mix_weight.shape, BF16),
                pltpu.VMEM((inner_columns // (2 * LANES), width, 2 * LANES), BF16),
                pltpu.VMEM((width, state_dim), BF16),
                pltpu.VMEM((width, state_dim), BF16),
                pltpu.VMEM((rows, width), BF16),
                pltpu.VMEM((max(sub_count - 1, 1), rows, width), BF16),
                pltpu.VMEM((rows, width), BF16),
                pltpu.VMEM((rows, inner_columns), BF16),
                pltpu.VMEM((rows // STRETCH, state_dim, heads * channels), F32),
                pltpu.VMEM((rows // STRETCH, heads, STRETCH, STRETCH), F32),
                pltpu.VMEM((rows // STRETCH, state_dim, heads * channels), BF16),
                pltpu.VMEM((state_dim, heads * channels), F32),
                pltpu.VMEM((state_pairs, LANES, state_dim), BF16),
                pltpu.VMEM((state_pairs, LANES, state_dim), BF16),
                dma((1,)),
                dma((1,)),
                dma((pieces, seq_count)),
                dma((pieces, seq_count)),
                dma((pieces, seq_count, grp_count)),
                dma((pieces, seq_count, grp_count)),
                dma((rows // STRIDE, sub_count)),
                dma((rows // STRIDE, sub_count)),
                dma((state_pairs,)),
                dma((state_pairs,)),
                dma((pieces + 6,)),
            ],
            compiler_params=pltpu.CompilerParams(
                collective_id=0, has_side_effects=True, vmem_limit_bytes=60 * 1024 * 1024
            ),
        )(
            queries,
            key_proj,
            value_proj,
            residual,
            mix_weight,
            inner_weight,
            write_weight,
            read_weight,
            jnp.transpose(step_logits, (1, 0, 2)),
            carried,
            decay_rates,
            carried_valid,
        )

    in_specs = (
        P(("grp", "seq"), "tm", "sub"),
        P(("grp", "seq"), "tm", "sub"),
        P(("grp", "seq"), "tm", "sub"),
        P(("grp", "seq"), "tm", None),
        P("sub", "seq"),
        P("seq", "sub"),
        P("seq", None),
        P("seq", None),
        P(("grp", "seq"), "sub", "tm"),
        P("sub"),
        P(("grp", "seq"), "sub", None, None),
        P(("grp", "seq"), "sub"),
    )
    out_specs = (P(("grp", "seq"), "tm", None), P(("grp", "seq"), "tm", "sub"))
    return jax.shard_map(
        on_device, mesh=mesh, in_specs=in_specs, out_specs=out_specs, check_vma=False
    )
```

```python
import functools

import jax
import jax.numpy as jnp
from jax import lax
from jax.experimental import pallas as pl
from jax.experimental.pallas import tpu as pltpu
from jax.sharding import PartitionSpec as P

MESH = pl.DeviceIdType.MESH
LANES = 128
HALF = 64
STRIDE = 256
STRETCH = 128
SCALE = 0.125
NEGATIVE = -1e30
EPSILON = 1e-05
F32 = jnp.float32
BF16 = jnp.bfloat16


def dot(a, b, contract=((1,), (0,)), precision=None):
    return lax.dot_general(
        a, b, (contract, ((), ())), precision=precision, preferred_element_type=F32
    )


def tile(index):
    return slice(index * LANES, (index + 1) * LANES)


def softplus(x):
    e = jnp.exp(-jnp.abs(x))
    u = 1.0 + e
    low = jnp.where(u == 1.0, e, jnp.log(u) * e / jnp.where(u == 1.0, 1.0, u - 1.0))
    return jnp.maximum(x, 0.0) + low


def layer(
    grp_count,
    tm_count,
    seq_count,
    sub_count,
    q_hbm,
    k_hbm,
    v_hbm,
    res_hbm,
    mix_ref,
    inw_ref,
    ww_ref,
    rw_ref,
    logit_hbm,
    carry_hbm,
    rates_ref,
    valid_ref,
    stream_ref,
    out_ref,
    q_ref,
    k_ref,
    v_ref,
    res_ref,
    logit_ref,
    carry_ref,
    strided,
    strided_sems,
    o_in,
    halo_out,
    halo_in,
    mixed,
    mix_all,
    inw_all,
    ww_all,
    rw_all,
    b_out,
    b_in,
    normed,
    inner,
    contrib,
    decays,
    states,
    first,
    s_out,
    s_in,
    h_send,
    h_recv,
    w_send,
    w_recv,
    f_send,
    f_recv,
    b_send,
    b_recv,
    s_send,
    s_recv,
    l_sem,
):
    me = lax.axis_index("tm")
    my_seq = lax.axis_index("seq")
    my_sub = lax.axis_index("sub")
    my_grp = lax.axis_index("grp")
    pairs = q_ref.shape[2] // LANES
    rows = q_ref.shape[1]
    width = res_ref.shape[2]
    share = STRIDE // tm_count
    heads = rates_ref.shape[0]
    state_pairs = heads // 2
    blocks = rows // STRETCH

    in_rows = inw_ref.shape[0]
    mine = pl.ds(pl.multiple_of(my_seq * in_rows, in_rows), in_rows)

    def peers(axis, mine, count):
        return [(d, {axis: lax.rem(mine + d, count)}) for d in range(1, count)]

    tm_peers = peers("tm", me, tm_count)
    seq_peers = peers("seq", my_seq, seq_count)
    sub_peers = peers("sub", my_sub, sub_count)
    grp_peers = peers("grp", my_grp, grp_count)
    barrier = pltpu.get_barrier_semaphore()
    hub = tm_count == 4
    greeted = seq_peers + sub_peers + grp_peers + ([] if hub else tm_peers)
    for _, peer in greeted:
        pl.semaphore_signal(barrier, inc=1, device_id=peer, device_id_type=MESH)
    arrivals = len(greeted)
    if hub:
        arrivals = arrivals + jnp.where(me == 0, 1, jnp.where(me == 1, 3, 2))
        for t in range(tm_count):
            apart = (me == t) | ((me == 0) & (t >= 2)) | ((me >= 2) & (t == 0))

            @pl.when(~apart)
            def _(t=t):
                pl.semaphore_signal(barrier, inc=1, device_id={"tm": t}, device_id_type=MESH)

    group = 2 * LANES
    groups = inw_ref.shape[1] // group
    moves = [("q", q_hbm, q_ref), ("k", k_hbm, k_ref), ("v", v_hbm, v_ref)]
    moves += [("mix", mix_ref, mix_all.at[my_seq])]
    moves += [("ww", ww_ref, ww_all.at[mine]), ("rw", rw_ref, rw_all.at[mine])]
    moves += [
        ("inw%d" % g, inw_ref.at[:, g * group : (g + 1) * group], inw_all.at[g, mine])
        for g in range(groups)
    ]
    moves += [("logit", logit_hbm, logit_ref), ("res", res_hbm, res_ref)]
    moves += [("carry", carry_hbm, carry_ref)]
    loads = {
        name: pltpu.make_async_copy(src, dst, l_sem.at[index])
        for index, (name, src, dst) in enumerate(moves)
    }
    for load in loads.values():
        load.start()
    loads["q"].wait()
    if not hub:
        loads["k"].wait()
        loads["v"].wait()
    low_half = lax.broadcasted_iota(jnp.int32, (STRIDE, LANES), 1) < HALF

    if hub:
        q_out, kv_out, q_in, kv_in, part_out, part_in, own_part = strided
        q_send, q_recv, kv_send, kv_recv, p_send, p_recv = strided_sems
    else:
        x_out, x_in, o_out = strided
        x_send, x_recv, o_send, o_recv = strided_sems

    def packed(ref, p):
        first_half = pltpu.roll(ref[0, :STRIDE, tile(p)].astype(F32), HALF, 1)
        second_half = ref[0, STRIDE:, tile(p)].astype(F32)
        return jnp.where(low_half, first_half, second_half).astype(BF16)

    for p in range(pairs):
        if hub:
            q_out[p] = packed(q_ref, p)
        else:
            for which, ref in enumerate((q_ref, k_ref, v_ref)):
                x_out[:, tile(which * pairs + p)] = packed(ref, p)

    def remote(src, dst, send, recv, peer):
        return pltpu.make_async_remote_copy(
            src_ref=src,
            dst_ref=dst,
            send_sem=send,
            recv_sem=recv,
            device_id=peer,
            device_id_type=MESH,
        )

    pl.semaphore_wait(barrier, arrivals)
    ahead = jnp.minimum(me + 1, tm_count - 1)
    if hub:
        asker = jnp.maximum(me - 2, 0)

        def q_copy(p, slot, to=1):
            sent = q_send.at[p] if to == 1 else q_send.at[pairs + p]
            return remote(q_out.at[p], q_in.at[slot, p], sent, q_recv.at[slot, p], {"tm": to})

        def kv_copy(p):
            return remote(kv_out.at[p], kv_in.at[p], kv_send.at[p], kv_recv.at[p], {"tm": 1})

        def part_copy(p, slot, to, place):
            return remote(
                part_out.at[slot, p],
                part_in.at[place, p],
                p_send.at[slot, p],
                p_recv.at[place, p],
                {"tm": to},
            )

        for p in range(pairs):

            @pl.when(me >= 2)
            def _(p=p):
                q_copy(p, asker).start()

        loads["k"].wait()
        loads["v"].wait()
        for p in range(pairs):
            kv_out[p, 0] = packed(k_ref, p)
            kv_out[p, 1] = packed(v_ref, p)

            @pl.when((me == 0) & (p < pairs - 1))
            def _(p=p):
                kv_copy(p).start()

    for p in range(pairs):
        key_tail = k_ref[0, rows - STRIDE :, tile(p)].astype(F32)
        value_tail = pltpu.roll(v_ref[0, rows - STRIDE :, tile(p)].astype(F32), HALF, 1)
        halo_out[:, tile(p)] = jnp.where(low_half, key_tail, value_tail).astype(BF16)

    @pl.when(me == 0)
    def _():
        halo_in[...] = jnp.zeros_like(halo_in)

    def residues(index):
        return pl.ds(pl.multiple_of(index * share, share), share)

    halo_copy = remote(halo_out, halo_in, h_send.at[0], h_recv.at[0], {"tm": ahead})
    if not hub:
        x_copies = [
            remote(
                x_out.at[residues(peer["tm"])], x_in.at[me], x_send.at[d], x_recv.at[d], peer
            )
            for d, peer in tm_peers
        ]
        for copy in x_copies:
            copy.start()

    @pl.when(me < tm_count - 1)
    def _():
        halo_copy.start()

    if hub:

        @pl.when(me == 0)
        def _():
            kv_copy(pairs - 1).start()

        for p in range(pairs):

            @pl.when(me == 3)
            def _(p=p):
                q_copy(p, 0, 2).start()

    pieces = ["mix", "ww", "rw"] + ["inw%d" % g for g in range(groups)]
    late = len(pieces) - 1
    halves = 2 if (in_rows // grp_count) % 32 == 0 else 1
    pieces += pieces[late:] * (halves - 1)

    def region(index, owner):
        if index == 0:
            part = mix_ref.shape[0] // grp_count
            return mix_all.at[owner, pl.ds(pl.multiple_of(my_grp * part, part), part)]
        part = in_rows // grp_count
        start = owner * in_rows + my_grp * part
        if index >= late:
            part = part // halves
            start = start + (index - late) * part
        at = pl.ds(pl.multiple_of(start, part), part)
        if index < 3:
            return (ww_all, rw_all)[index - 1].at[at]
        return inw_all.at[min(index, late) - 3, at]

    w_copies, f_copies = [], []
    for index, name in enumerate(pieces):
        if index <= late:
            loads[name].wait()
        own = region(index, my_seq)
        w_copies.append(
            [
                remote(own, own, w_send.at[index, d], w_recv.at[index, d], peer)
                for d, peer in seq_peers
            ]
        )
        f_copies.append([])
        for d, _ in seq_peers:
            place = region(index, lax.rem(my_seq - d + seq_count, seq_count))
            for e, peer in grp_peers:
                f_copies[-1].append(
                    remote(place, place, f_send.at[index, d, e], f_recv.at[index, d, e], peer)
                )
        for copy in w_copies[-1]:
            copy.start()

    def pass_on(index):
        for copy in w_copies[index]:
            copy.wait()
        for copy in f_copies[index]:
            copy.start()

    if not hub:
        x_in[me] = x_out[residues(me), :]

    row_at = lax.broadcasted_iota(jnp.int32, (STRIDE, STRIDE), 0)
    col_at = lax.broadcasted_iota(jnp.int32, (STRIDE, STRIDE), 1)
    own_allowed = col_at <= row_at

    def near(block, prev_keys, prev_values, prev_allowed, turned):
        at = slice(block * STRIDE, (block + 1) * STRIDE)
        for p in range(pairs):
            query = jnp.where(low_half, q_ref[0, at, tile(p)].astype(F32) * SCALE, 0.0).astype(BF16)
            own = dot(query, k_ref[0, at, tile(p)], ((1,), (1,)))
            prev = dot(query, prev_keys(p), ((1,), (1,)))
            own = jnp.where(own_allowed, own, NEGATIVE)
            prev = jnp.where(prev_allowed, prev, NEGATIVE)
            top = jnp.maximum(
                jnp.max(own, axis=1, keepdims=True), jnp.max(prev, axis=1, keepdims=True)
            )
            own = jnp.where(own_allowed, jnp.exp(own - top), 0.0)
            prev = jnp.where(prev_allowed, jnp.exp(prev - top), 0.0)
            total = jnp.sum(own, axis=1, keepdims=True) + jnp.sum(prev, axis=1, keepdims=True)
            from_prev = dot(prev.astype(BF16), prev_values(p))
            if turned:
                from_prev = pltpu.roll(from_prev, HALF, 1)
            result = dot(own.astype(BF16), v_ref[0, at, tile(p)]) + from_prev
            mixed[at, tile(p)] = (result / total).astype(BF16)

    def first_block():
        @pl.when(me > 0)
        def _():
            halo_copy.wait_recv()

        near(
            0,
            lambda p: halo_in[:, tile(p)],
            lambda p: halo_in[:, tile(p)],
            (col_at > row_at) & (me > 0),
            True,
        )

    near(
        1,
        lambda p: k_ref[0, :STRIDE, tile(p)],
        lambda p: v_ref[0, :STRIDE, tile(p)],
        col_at > row_at,
        False,
    )

    loads["logit"].wait()
    head_at = lax.broadcasted_iota(jnp.int32, (heads, 1), 0)
    rates = jnp.zeros((heads, 1), F32)
    flags = jnp.zeros((heads, 1), F32)
    for h in range(heads):
        rates = jnp.where(head_at == h, rates_ref[h], rates)
        flags = jnp.where(head_at == h, valid_ref[0, h].astype(F32), flags)
    step = softplus(logit_ref[:, 0, :])
    log_decay = -rates * step
    tri = (
        lax.broadcasted_iota(jnp.int32, (STRETCH, STRETCH), 0)
        <= lax.broadcasted_iota(jnp.int32, (STRETCH, STRETCH), 1)
    ).astype(F32)
    step_rows, cum_rows, cum_cols, grow_cols, tail_cols, block_decay = [], [], [], [], [], []
    for c in range(blocks):
        at = slice(c * STRETCH, (c + 1) * STRETCH)
        cum = dot(log_decay[:, at], tri, precision=lax.Precision.HIGHEST)
        last = cum[:, STRETCH - 1 :]
        tail = jnp.exp(last - cum) * step[:, at]
        step_rows.append(step[:, at])
        cum_rows.append(cum)
        cum_cols.append(jnp.transpose(cum))
        grow_cols.append(jnp.exp(cum_cols[-1]))
        tail_cols.append(jnp.transpose(tail))
        block_decay.append(jnp.exp(last))

    low_lane = lax.broadcasted_iota(jnp.int32, (STRETCH, LANES), 1) < HALF
    low_row = low_lane[:1]

    def over_lanes(entries, pair):
        return jnp.where(low_row, entries[2 * pair : 2 * pair + 1], entries[2 * pair + 1 : 2 * pair + 2])

    loads["carry"].wait()
    for pair in range(state_pairs):
        valid = over_lanes(flags, pair) != 0.0
        first[:, tile(pair)] = jnp.where(valid, jnp.transpose(carry_ref[0, tile(pair), :]), 0.0)

    causal = lax.broadcasted_iota(jnp.int32, (STRETCH, STRETCH), 0) >= lax.broadcasted_iota(
        jnp.int32, (STRETCH, STRETCH), 1
    )
    for c in range(blocks):
        for h in range(heads):
            distance = cum_cols[c][:, h : h + 1] - cum_rows[c][h : h + 1, :]
            decay = jnp.exp(jnp.where(causal, distance, NEGATIVE))
            decays[c, h] = decay * step_rows[c][h : h + 1, :]

    pass_on(0)
    if not hub:
        for index in range(1, len(pieces)):
            pass_on(index)
        for copy in x_copies:
            copy.wait()
    ones = (
        (lax.broadcasted_iota(jnp.int32, (LANES, LANES), 0) < HALF)
        == (lax.broadcasted_iota(jnp.int32, (LANES, LANES), 1) < HALF)
    ).astype(BF16)
    if hub:
        upper = ~low_half
        stat_row = lax.broadcasted_iota(jnp.int32, (16, 3 * LANES), 0)
        stat_lane = lax.broadcasted_iota(jnp.int32, (16, 3 * LANES), 1)
        stat_pick = (
            (stat_row < 6) & (stat_lane == (stat_row // 2) * LANES + (stat_row % 2) * HALF)
        ).astype(BF16)
        back_row = lax.broadcasted_iota(jnp.int32, (16, LANES), 0)
        back_low = lax.broadcasted_iota(jnp.int32, (16, LANES), 1) < HALF
        stat_back = ((back_row < 6) & ((back_row % 2 == 0) == back_low)).astype(BF16)

        def lane_sums(product):
            high = product.astype(BF16)
            low = (product - high.astype(F32)).astype(BF16)
            return dot(high, ones) + dot(low, ones)

        def with_turned(ref, p):
            keys, values = ref[p, 0].astype(F32), ref[p, 1].astype(F32)
            return keys, pltpu.roll(keys, HALF, 1), values, pltpu.roll(values, HALF, 1)

        def attend(query, sets, diagonal):
            scores = []
            for index, (keys, keys_turned, _, _) in enumerate(sets):
                straight, turned = lane_sums(keys * query), lane_sums(keys_turned * query)
                if diagonal and index == 0:
                    turned = jnp.where(upper, turned, NEGATIVE)
                scores.append((straight, turned))
            top = functools.reduce(jnp.maximum, [jnp.maximum(*pair) for pair in scores])
            total, result = 0.0, 0.0
            for index, (_, _, values, values_turned) in enumerate(sets):
                straight, turned = (jnp.exp(entry - top) for entry in scores[index])
                if diagonal and index == 0:
                    turned = jnp.where(upper, turned, 0.0)
                total = total + (straight + turned)
                result = result + (
                    straight.astype(BF16).astype(F32) * values
                    + turned.astype(BF16).astype(F32) * values_turned
                )
            return result, total, top

        def keep(p, sets):
            outcome = attend(q_out[p].astype(F32) * SCALE, sets, True)
            for index, entry in enumerate(outcome):
                own_part[index, p] = entry

        def serve(p, slot, sets, to, place):
            q_copy(p, slot).wait_recv()
            result, total, top = attend(q_in[slot, p].astype(F32) * SCALE, sets, False)
            part_out[slot, p, :STRIDE] = (result / total).astype(BF16)
            log_sum = top + jnp.log(total)
            high = log_sum.astype(BF16)
            left = log_sum - high.astype(F32)
            middle = left.astype(BF16)
            low = (left - middle.astype(F32)).astype(BF16)
            stats = dot(
                stat_pick, jnp.concatenate([high, middle, low], axis=1), ((1,), (1,))
            ).astype(BF16)
            part_out[slot, p, STRIDE : STRIDE + 16] = stats[:, :LANES]
            part_out[slot, p, STRIDE + 16 :] = stats[:, LANES:]
            part_copy(p, slot, to, place).start()

        pass_at = {0: (1, 2)}
        for p in range(pairs):
            if p == pairs - 1:
                first_block()
                pass_on(3)

            @pl.when(me == 1)
            def _(p=p):
                kv_copy(p).wait_recv()
                sets = (with_turned(kv_out, p), with_turned(kv_in, p))
                for slot in range(2):
                    serve(p, slot, sets, 2 + slot, 0)
                keep(p, sets)

            @pl.when(me == 2)
            def _(p=p):
                sets = (with_turned(kv_out, p),)
                serve(p, 0, sets, 3, 1)
                keep(p, sets)

            @pl.when((me == 0) | (me == 3))
            def _(p=p):
                keep(p, (with_turned(kv_out, p),))

            for index in pass_at.get(p, ()):
                pass_on(index)
    else:
        source = lax.broadcasted_iota(jnp.int32, (tm_count, share, LANES), 0)
        upper = lax.broadcasted_iota(jnp.int32, (tm_count, share, LANES), 2) >= HALF
        full = (tm_count * share, LANES)
        cube = (tm_count, share, LANES)

        def lane_sums(product):
            product = product.reshape(full)
            high = product.astype(BF16)
            low = (product - high.astype(F32)).astype(BF16)
            return (dot(high, ones) + dot(low, ones)).reshape(cube)

        o_copies = []
        for p in range(pairs):
            keys = x_in[:, :, tile(pairs + p)].astype(F32)
            values = x_in[:, :, tile(2 * pairs + p)].astype(F32)
            keys_turned = pltpu.roll(keys.reshape(full), HALF, 1).reshape(cube)
            values_turned = pltpu.roll(values.reshape(full), HALF, 1).reshape(cube)

            def far(d, carry, p=p, keys=keys, values=values, kt=keys_turned, vt=values_turned):
                query = x_in[d, :, tile(p)].astype(F32)[None] * SCALE
                allowed = source <= d
                allowed_turned = (source < d) | ((source == d) & upper)
                straight = jnp.where(allowed, lane_sums(keys * query), NEGATIVE)
                turned = jnp.where(allowed_turned, lane_sums(kt * query), NEGATIVE)
                top = jnp.max(jnp.maximum(straight, turned), axis=0, keepdims=True)
                straight = jnp.where(allowed, jnp.exp(straight - top), 0.0)
                turned = jnp.where(allowed_turned, jnp.exp(turned - top), 0.0)
                total = jnp.sum(straight + turned, axis=0)
                result = jnp.sum(
                    straight.astype(BF16).astype(F32) * values + turned.astype(BF16).astype(F32) * vt,
                    axis=0,
                )
                o_out[d, :, tile(p)] = (result / total).astype(BF16)
                return carry

            lax.fori_loop(0, tm_count, far, 0, unroll=tm_count <= 4)

            for d, peer in tm_peers:
                o_copies.append(
                    remote(
                        o_out.at[peer["tm"], :, tile(p)],
                        o_in.at[residues(me), tile(p)],
                        o_send.at[p, d],
                        o_recv.at[p, d],
                        peer,
                    )
                )
                o_copies[-1].start()

        o_in[residues(me), :] = o_out[me]

    if not hub:
        first_block()
    if hub:
        for index in range(4, late):
            pass_on(index)
        for p in range(pairs):
            if p == pairs - 1:

                @pl.when(me >= 2)
                def _():
                    for index in range(late, len(pieces)):
                        pass_on(index)


            @pl.when(me < 2)
            def _(p=p):
                o_in[:, tile(p)] = (own_part[0, p] / own_part[1, p]).astype(BF16)

            for count, condition in ((1, me == 2), (2, me == 3)):

                @pl.when(condition)
                def _(p=p, count=count):
                    log_sums = []
                    for place in range(count):
                        part_copy(p, 0, 2, place).wait_recv()
                        halves = [
                            part_in[place, p, STRIDE + 16 * half : STRIDE + 16 * (half + 1)]
                            for half in range(2)
                        ]
                        log_sums.append(
                            jnp.concatenate(
                                [dot(half, stat_back, ((0,), (0,))) for half in halves], axis=0
                            )
                        )
                    top = functools.reduce(jnp.maximum, log_sums, own_part[2, p])
                    scale = jnp.exp(own_part[2, p] - top)
                    result, total = own_part[0, p] * scale, own_part[1, p] * scale
                    for place in range(count):
                        scale = jnp.exp(log_sums[place] - top)
                        result = result + part_in[place, p, :STRIDE].astype(F32) * scale
                        total = total + scale
                    o_in[:, tile(p)] = (result / total).astype(BF16)
    else:
        for copy in o_copies:
            copy.wait()
    for copy in f_copies[0]:
        copy.wait()

    piece = mix_ref.shape[1]
    b_copies = []
    for a in range(rows // STRIDE):
        at = slice(a * STRIDE, (a + 1) * STRIDE)
        for p in range(pairs):
            far_part = o_in[:, tile(p)].astype(F32)
            if a == 0:
                far_part = pltpu.roll(far_part, HALF, 1)
            mixed[at, tile(p)] = jnp.where(
                low_half, mixed[at, tile(p)].astype(F32), far_part
            ).astype(BF16)
        if piece % LANES == 0:
            for s in range(seq_count):
                b_out[at, s * piece : (s + 1) * piece] = dot(mixed[at, :], mix_all[s]).astype(BF16)
        else:
            total = jnp.zeros((STRIDE, width), F32)
            from_col = lax.broadcasted_iota(jnp.int32, (piece, width), 0)
            to_col = lax.broadcasted_iota(jnp.int32, (piece, width), 1)
            for s in range(seq_count):
                placed = (to_col == from_col + s * piece).astype(BF16)
                weight = dot(mix_all[s], placed).astype(BF16)
                total = total + dot(mixed[at, :], weight)
            b_out[at, :] = total.astype(BF16)
        b_copies.append(
            [
                remote(
                    b_out.at[pl.ds(a * STRIDE, STRIDE)],
                    b_in.at[d - 1, pl.ds(a * STRIDE, STRIDE)],
                    b_send.at[a, d],
                    b_recv.at[a, d],
                    peer,
                )
                for d, peer in sub_peers
            ]
        )
        for copy in b_copies[-1]:
            copy.start()
    if hub:

        @pl.when(me < 2)
        def _():
            for index in range(late, len(pieces)):
                pass_on(index)

    loads["res"].wait()
    for index in (1, 2):
        for copy in f_copies[index]:
            copy.wait()
    read_vecs, write_vecs, write_turned = [], [], []
    for a in range(rows // STRIDE):
        at = slice(a * STRIDE, (a + 1) * STRIDE)
        for copy in b_copies[a]:
            copy.wait()
        branch = b_out[at, :].astype(F32)
        for d, _ in sub_peers:
            branch = branch + b_in[d - 1, at, :].astype(F32)
        stream = (res_ref[0, at, :].astype(F32) + branch).astype(BF16)
        stream_ref[0, at, :] = stream
        wide = stream.astype(F32)
        mean = jnp.sum(wide * wide, axis=1, keepdims=True) * (1.0 / width)
        normed[at, :] = (wide * lax.rsqrt(mean + EPSILON)).astype(BF16)
        write_vec = dot(normed[at, :], ww_all[...]).astype(BF16)
        read_vec = dot(normed[at, :], rw_all[...]).astype(BF16)
        for c in range(STRIDE // STRETCH):
            write_vecs.append(write_vec[c * STRETCH : (c + 1) * STRETCH])
            write_turned.append(jnp.transpose(write_vecs[-1].astype(F32)).astype(BF16))
            read_vecs.append(read_vec[c * STRETCH : (c + 1) * STRETCH])
    def by_lane(cols, pair):
        return jnp.where(
            low_lane, cols[:, 2 * pair : 2 * pair + 1], cols[:, 2 * pair + 1 : 2 * pair + 2]
        )

    def s_copy(pair):
        return remote(
            s_out.at[pair], s_in.at[pair], s_send.at[pair], s_recv.at[pair], {"tm": ahead}
        )

    def take_state(pair):
        @pl.when(me > 0)
        def _():
            s_copy(pair).wait_recv()

        @pl.when(me == 0)
        def _():
            s_in[pair] = first[:, tile(pair)].astype(BF16)

        state = jnp.where(me == 0, first[:, tile(pair)], s_in[pair].astype(F32))
        for c in range(blocks):
            states[c, :, tile(pair)] = state.astype(BF16)
            state = over_lanes(block_decay[c], pair) * state + contrib[c, :, tile(pair)]
        s_out[pair] = state.astype(BF16)

    for g in range(groups):
        columns = slice(g * group, (g + 1) * group)
        for index in range(3 + g, 4 + g if 3 + g < late else len(pieces)):
            for copy in f_copies[index]:
                copy.wait()
        for a in range(rows // STRIDE):
            at = slice(a * STRIDE, (a + 1) * STRIDE)
            drive = dot(normed[at, :], inw_all[g])
            inner[at, columns] = (drive / (1.0 + jnp.exp(-drive))).astype(BF16)
        for c in range(blocks):
            at = slice(c * STRETCH, (c + 1) * STRETCH)
            tails = jnp.concatenate([by_lane(tail_cols[c], pair) for pair in (2 * g, 2 * g + 1)], axis=1)
            weighted = (inner[at, columns].astype(F32) * tails).astype(BF16)
            contrib[c, :, columns] = dot(write_turned[c], weighted)

        @pl.when(me < tm_count - 1)
        def _(g=g):
            for pair in (2 * g, 2 * g + 1):
                take_state(pair)
                s_copy(pair).start()

    grams = [dot(read_vecs[c], write_vecs[c], ((1,), (1,))) for c in range(blocks)]

    def within_of(pair):
        within = []
        for c in range(blocks):
            at = slice(c * STRETCH, (c + 1) * STRETCH)
            entries = inner[at, tile(pair)]
            parts = []
            for h in (2 * pair, 2 * pair + 1):
                matrix = decays[c, h] * grams[c]
                parts.append(dot(matrix.astype(BF16), entries))
            within.append(jnp.where(low_lane, parts[0], parts[1]))
        return within

    ready = [within_of(pair) for pair in range(state_pairs)]
    for pair in range(state_pairs):

        @pl.when(me == tm_count - 1)
        def _(pair=pair):
            take_state(pair)

        for c in range(blocks):
            at = slice(c * STRETCH, (c + 1) * STRETCH)
            carried = dot(read_vecs[c], states[c, :, tile(pair)]) * by_lane(grow_cols[c], pair)
            out_ref[0, at, tile(pair)] = (ready[pair][c] + carried).astype(BF16)

    @pl.when(me < tm_count - 1)
    def _():
        halo_copy.wait_send()
        for pair in range(state_pairs):
            s_copy(pair).wait_send()

    if hub:
        for p in range(pairs):

            @pl.when(me >= 2)
            def _(p=p):
                q_copy(p, asker).wait_send()

            @pl.when(me == 3)
            def _(p=p):
                q_copy(p, 0, 2).wait_send()

            @pl.when(me == 0)
            def _(p=p):
                kv_copy(p).wait_send()

            @pl.when((me == 1) | (me == 2))
            def _(p=p):
                part_copy(p, 0, 3, 0).wait_send()

            @pl.when(me == 1)
            def _(p=p):
                part_copy(p, 1, 3, 0).wait_send()


def solution(mesh):
    grp_count, tm_count, seq_count, sub_count = (
        mesh.shape[axis] for axis in ("grp", "tm", "seq", "sub")
    )

    def on_device(
        queries,
        key_proj,
        value_proj,
        residual,
        mix_weight,
        inner_weight,
        write_weight,
        read_weight,
        step_logits,
        decay_rates,
        carried_state,
        carried_valid,
    ):
        rows, columns = queries.shape[1:]
        width = residual.shape[2]
        heads, channels, state_dim = carried_state.shape[1:]
        assert rows == 2 * STRIDE and state_dim == LANES and channels == HALF
        pairs = columns // LANES
        share = STRIDE // tm_count
        inner_columns = inner_weight.shape[1]
        state_pairs = heads // 2
        carried = carried_state.reshape(1, heads * channels, state_dim)
        vmem = pl.BlockSpec(memory_space=pltpu.VMEM)
        smem = pl.BlockSpec(memory_space=pltpu.SMEM)
        anywhere = pl.BlockSpec(memory_space=pl.ANY)
        dma = pltpu.SemaphoreType.DMA
        pieces = 3 + inner_columns // (2 * LANES)
        if tm_count == 4:
            strided = (
                pltpu.VMEM((pairs, STRIDE, LANES), BF16),
                pltpu.VMEM((pairs, 2, STRIDE, LANES), BF16),
                pltpu.VMEM((2, pairs, STRIDE, LANES), BF16),
                pltpu.VMEM((pairs, 2, STRIDE, LANES), BF16),
                pltpu.VMEM((2, pairs, STRIDE + 32, LANES), BF16),
                pltpu.VMEM((2, pairs, STRIDE + 32, LANES), BF16),
                pltpu.VMEM((3, pairs, STRIDE, LANES), F32),
            )
            strided_sems = tuple(
                dma(extent)
                for extent in ((2 * pairs,), (2, pairs), (pairs,), (pairs,), (2, pairs), (2, pairs))
            )
        else:
            strided = (
                pltpu.VMEM((STRIDE, 3 * columns), BF16),
                pltpu.VMEM((tm_count, share, 3 * columns), BF16),
                pltpu.VMEM((tm_count, share, columns), BF16),
            )
            strided_sems = tuple(
                dma(extent)
                for extent in ((tm_count,), (tm_count,), (pairs, tm_count), (pairs, tm_count))
            )
        return pl.pallas_call(
            functools.partial(layer, grp_count, tm_count, seq_count, sub_count),
            out_shape=(
                pltpu.VMEM((1, rows, width), BF16),
                pltpu.VMEM((1, rows, inner_columns), BF16),
            ),
            in_specs=[anywhere] * 10 + [smem] * 2,
            out_specs=(vmem, vmem),
            scratch_shapes=[
                pltpu.VMEM((1, rows, columns), BF16),
                pltpu.VMEM((1, rows, columns), BF16),
                pltpu.VMEM((1, rows, columns), BF16),
                pltpu.VMEM((1, rows, width), BF16),
                pltpu.VMEM((heads, 1, rows), F32),
                pltpu.VMEM((1, heads * channels, state_dim), F32),
                strided,
                strided_sems,
                pltpu.VMEM((STRIDE, columns), BF16),
                pltpu.VMEM((STRIDE, columns), BF16),
                pltpu.VMEM((STRIDE, columns), BF16),
                pltpu.VMEM((rows, columns), BF16),
                pltpu.VMEM((seq_count,) + mix_weight.shape, BF16),
                pltpu.VMEM((inner_columns // (2 * LANES), width, 2 * LANES), BF16),
                pltpu.VMEM((width, state_dim), BF16),
                pltpu.VMEM((width, state_dim), BF16),
                pltpu.VMEM((rows, width), BF16),
                pltpu.VMEM((max(sub_count - 1, 1), rows, width), BF16),
                pltpu.VMEM((rows, width), BF16),
                pltpu.VMEM((rows, inner_columns), BF16),
                pltpu.VMEM((rows // STRETCH, state_dim, heads * channels), F32),
                pltpu.VMEM((rows // STRETCH, heads, STRETCH, STRETCH), F32),
                pltpu.VMEM((rows // STRETCH, state_dim, heads * channels), BF16),
                pltpu.VMEM((state_dim, heads * channels), F32),
                pltpu.VMEM((state_pairs, LANES, state_dim), BF16),
                pltpu.VMEM((state_pairs, LANES, state_dim), BF16),
                dma((1,)),
                dma((1,)),
                dma((pieces + 1, seq_count)),
                dma((pieces + 1, seq_count)),
                dma((pieces + 1, seq_count, grp_count)),
                dma((pieces + 1, seq_count, grp_count)),
                dma((rows // STRIDE, sub_count)),
                dma((rows // STRIDE, sub_count)),
                dma((state_pairs,)),
                dma((state_pairs,)),
                dma((pieces + 6,)),
            ],
            compiler_params=pltpu.CompilerParams(
                collective_id=0, has_side_effects=True, vmem_limit_bytes=60 * 1024 * 1024
            ),
        )(
            queries,
            key_proj,
            value_proj,
            residual,
            mix_weight,
            inner_weight,
            write_weight,
            read_weight,
            jnp.transpose(step_logits, (1, 0, 2)),
            carried,
            decay_rates,
            carried_valid,
        )

    in_specs = (
        P(("grp", "seq"), "tm", "sub"),
        P(("grp", "seq"), "tm", "sub"),
        P(("grp", "seq"), "tm", "sub"),
        P(("grp", "seq"), "tm", None),
        P("sub", "seq"),
        P("seq", "sub"),
        P("seq", None),
        P("seq", None),
        P(("grp", "seq"), "sub", "tm"),
        P("sub"),
        P(("grp", "seq"), "sub", None, None),
        P(("grp", "seq"), "sub"),
    )
    out_specs = (P(("grp", "seq"), "tm", None), P(("grp", "seq"), "tm", "sub"))
    return jax.shard_map(
        on_device, mesh=mesh, in_specs=in_specs, out_specs=out_specs, check_vma=False
    )
```
